32 devices in a mesh: grp: 2 (over x), node: 16 (over z, y, core).
Axes of the slice: x: 2, y: 2, z: 4, core: 2. Of those that a mesh axis runs over, the one named last changes fastest.
Arguments:
- nodes: bfloat16 [128, 2, 1024, 1024], P('grp', None, 'node'), parts along dimension 0, may hold values from -0.34960938 to 0.34960938
- pair_nodes: int32 [16, 2], replicated, may hold values from 0 to 63
- prod_left: int32 [16], replicated, may hold values from 0 to 15, as said below
- prod_right: int32 [16], replicated, may hold values from 0 to 15, each once
- prod_flag: int32 [16], replicated, may hold values from 0 to 1
- prod_diag: int32 [16], replicated, may hold values from 0 to 7, as said below
Outputs:
- diagrams: bfloat16 [16, 2, 1024, 1024], P('grp', None, 'node'), parts along dimension 0
The draws below stay inside these ranges and needn't reach their ends.
There are 2 independent parts, one for each index of `grp`. The reference program is written for one: setup_inputs(seed, part) draws one part's arguments, and reference() takes and returns one part's arrays. A program takes and returns all parts, laid end to end along the dimension named above; an argument that names none is the same for every part. Nothing has to cross between parts.
Inputs may be any that keep to these rules, and one draw needn't show every extreme that they name: `prod_left`: exactly 8 distinct pairs are left operands, each of exactly two products. `prod_diag`: every diagram receives exactly two products.
All inputs are finite; a program needn't handle non-finite values.
Results may differ from the reference program's by a relative error of at most 0.0065.
Values may be sent and summed in bfloat16 or wider, within the bound.
A program may use at most 128 MiB of HBM per device.

```python
import jax
import jax.numpy as jnp
from jax import lax

M = 1024
NODES = 64
PAIRS = 16
PRODS = 16
DIAGS = 8


def draw_prod_left(key, part):
    base = jax.random.permutation(jax.random.fold_in(key, 11), PAIRS).astype(jnp.int32)
    return base[jnp.arange(PRODS, dtype=jnp.int32) // 2].astype(jnp.int32)


def draw_prod_diag(key, part):
    order = jax.random.permutation(jax.random.fold_in(key, 23), PRODS).astype(jnp.int32)
    return (order % DIAGS).astype(jnp.int32)


def plant(result, key, low, top_value):
    longest = result.shape.index(max(result.shape))
    spots = []
    for shift in (0, 1):
        where = [jax.random.randint(jax.random.fold_in(key, axis), (), 0, length) for axis, length in enumerate(result.shape)]
        where[longest] = (where[longest] + shift) % result.shape[longest]
        spots.append(tuple(where))
    return result.at[spots[0]].set(low).at[spots[1]].set(top_value)


def steps_of(stream_key, shape, shards, low, top_value):
    gain = 1.0
    for position, blocks in shards:
        draws = jax.random.uniform(jax.random.fold_in(jax.random.fold_in(stream_key, 6), position), (blocks,), jnp.float32, low / len(shards), top_value / len(shards))
        gain = gain * jnp.repeat(jnp.exp(draws), shape[position] // blocks).reshape((-1,) + (1,) * (len(shape) - 1 - position))
    return gain


def noise(own_key, shape, spread, bound, pieces=(), held_as=jnp.bfloat16):
    array = spread * jax.random.normal(own_key, shape, jnp.float32)
    if pieces:
        array = array * steps_of(own_key, shape, pieces, -0.22, 0.18)
    return jnp.clip(array, -bound, bound).astype(held_as)


def setup_inputs(seed: int = 0, part: int = 0) -> dict:
    keys = jax.random.split(jax.random.key(seed), 7)
    own_keys = jax.random.split(jax.random.fold_in(keys[6], part), 7)
    return {
        "nodes": noise(own_keys[0], (NODES, 2, M, M), 0.0573, 0.34960938, ((2, 16),)),
        "pair_nodes": plant(jax.random.randint(keys[1], (PAIRS, 2), 0, NODES), jax.random.fold_in(keys[1], 1), 0, NODES - 1).astype(jnp.int32),
        "prod_left": draw_prod_left(jax.random.fold_in(keys[6], 71), part),
        "prod_right": jax.random.permutation(keys[3], PAIRS).astype(jnp.int32),
        "prod_flag": plant(jax.random.randint(keys[4], (PRODS,), 0, 2), jax.random.fold_in(keys[4], 1), 0, 1).astype(jnp.int32),
        "prod_diag": draw_prod_diag(jax.random.fold_in(keys[6], 71), part),
    }


def complex_product(left_re, left_im, right_re, right_im):
    real_part = jnp.dot(left_re, right_re, preferred_element_type=jnp.float32) - jnp.dot(left_im, right_im, preferred_element_type=jnp.float32)
    imag_part = jnp.dot(left_re, right_im, preferred_element_type=jnp.float32) + jnp.dot(left_im, right_re, preferred_element_type=jnp.float32)
    return jnp.stack([real_part, imag_part]).astype(jnp.bfloat16)


def reference(nodes, pair_nodes, prod_left, prod_right, prod_flag, prod_diag):
    def pair_one(entry):
        left_node = nodes[entry[0]]
        right_node = nodes[entry[1]]
        return complex_product(left_node[0], left_node[1], right_node[0], right_node[1])

    paired = lax.map(pair_one, pair_nodes)

    def second_one(entry):
        left_pair = paired[entry[0]]
        right_pair = paired[entry[1]]
        flipped = entry[2] == 1
        left_re = jnp.where(flipped, left_pair[0].T, left_pair[0])
        left_im = jnp.where(flipped, -left_pair[1].T, left_pair[1])
        return complex_product(left_re, left_im, right_pair[0], right_pair[1])

    entries = jnp.stack([prod_left, prod_right, prod_flag], axis=1)
    results = lax.map(second_one, entries)
    diagram_map = (prod_diag[None, :] == jnp.arange(DIAGS, dtype=jnp.int32)[:, None]).astype(jnp.float32)
    summed = jnp.dot(diagram_map, results.reshape(PRODS, -1).astype(jnp.float32), precision=lax.Precision.HIGHEST)
    return summed.reshape(DIAGS, 2, M, M).astype(jnp.bfloat16)
```

```python
import functools

import jax
import jax.numpy as jnp
from jax import lax
from jax.experimental import pallas as pl
from jax.experimental.pallas import tpu as pltpu
from jax.sharding import PartitionSpec as P

TILE = 256
AHEAD = 8
WIDTH = 128
BAND = 16
LANES = 128


def searched(count):
    return 2 ** (count // 2 - 1) <= LANES


def plan_sizes(count):
    groups = count // 2
    if searched(count):
        return 3 * groups // 4, 3 * groups // 4
    return groups, groups


def choose_sides(graph, product, home, sides, group_of, extra, slots):
    groups = sides.shape[0]
    count = 2 * groups
    half = groups
    lane = lax.broadcasted_iota(jnp.int32, sides.shape, 1)
    group = lax.broadcasted_iota(jnp.int32, sides.shape, 0)
    sides[...] = lax.rem(lax.shift_right_logical(lane, group), 2).astype(jnp.float32)
    row = lambda g: sides[pl.ds(g, 1), :]
    zero = jnp.zeros((1, sides.shape[1]), jnp.float32)

    def add_group(g, carry):
        ones, inside_0, inside_1 = carry
        here = row(g)
        there = row(group_of[home[graph[2, product[2 * g]]]])
        return ones + here, inside_0 + (1 - here) * (1 - there), inside_1 + here * there

    ones, inside_0, inside_1 = lax.fori_loop(0, groups, add_group, (zero, zero, zero))

    def add_diag(k, carry):
        own_0, own_1 = carry
        k_mate = product[count + k]
        here, there = row(group_of[k]), row(group_of[k_mate])
        first = (k < k_mate).astype(jnp.float32)
        return own_0 + first * (1 - here * there), own_1 + first * jnp.maximum(here, there)

    own_0, own_1 = lax.fori_loop(0, count, add_diag, (zero, zero))
    new = half - jnp.minimum(inside_0, inside_1)
    own = jnp.maximum(own_0, own_1)
    bad = jnp.where(ones != groups // 2, 4096.0, 0.0)
    bad = bad + jnp.where(new > extra, 256.0, 0.0) + jnp.where(own > slots, 256.0, 0.0)
    cost = bad + 2 * new + own
    best = jnp.min(cost)
    index = lax.broadcasted_iota(jnp.int32, cost.shape, 1).astype(jnp.float32)
    return jnp.min(jnp.where(cost == best, index, 1e9)).astype(jnp.int32)


def plan_and_gather_kernel(
    n,
    graph,
    nodes,
    flags,
    left_slot,
    extra_slot,
    is_extra,
    merges,
    finals,
    left_own,
    a_own,
    b_own,
    left_cross,
    a_cross,
    b_cross,
    seen,
    group_of,
    product,
    home,
    chip_of,
    extras,
    used,
    slot_of,
    order,
    sides,
    early_sem,
    late_sem,
):
    count = graph.shape[1]
    groups = diags = half = count // 2
    extra = a_cross.shape[0]
    slots = merges.shape[0] // 4
    chunks = b_own.shape[0]
    width = b_own.shape[-1]
    first_node, prod_left, prod_right, prod_flag, prod_diag = 0, 2, 3, 4, 5
    me = lax.axis_index("node")
    side = lax.div(me, n // 2)

    @pl.loop(0, count)
    def _(p):
        seen[p] = -1
        seen[count + p] = -1
        chip_of[p] = -1

    @pl.loop(0, 2 * extra)
    def _(e):
        extras[e] = 0

    @pl.loop(0, 2 * diags)
    def _(d):
        slot_of[d] = -1

    def read(k, found):
        left = graph[prod_left, k]
        new = seen[left] < 0
        group = jnp.where(new, found, seen[left])
        seen[left] = group
        group_of[k] = group
        product[2 * group + 1] = k
        product[2 * group] = jnp.where(new, k, product[2 * group])
        home[graph[prod_right, k]] = k
        diag = graph[prod_diag, k]
        earlier = seen[count + diag]
        seen[count + diag] = k
        back = jnp.where(earlier < 0, k, earlier)
        product[count + k] = back
        product[count + back] = k
        return found + new.astype(jnp.int32)

    lax.fori_loop(0, count, read, jnp.int32(0))

    if not searched(count):
        mask = jnp.int32(2 ** (groups // 2) - 1)
    else:
        mask = choose_sides(graph, product, home, sides, group_of, extra, slots)

    def place(g, counts):
        which = lax.rem(lax.shift_right_logical(mask, g), 2)
        chip = jnp.where(which == 0, counts[0], groups // 2 + counts[1])
        order[2 * chip] = product[2 * g]
        order[2 * chip + 1] = product[2 * g + 1]
        chip_of[graph[prod_left, product[2 * g]]] = chip
        return counts[0] + 1 - which, counts[1] + which

    lax.fori_loop(0, groups, place, (jnp.int32(0), jnp.int32(0)))

    def read_node(node, dst, sem):
        pltpu.make_async_copy(nodes.at[node], dst, sem).start()

    def read_chunks(node, dst, at):
        for c in range(chunks):
            pltpu.make_async_copy(
                nodes.at[node, :, :, pl.ds(c * width, width)], dst.at[c, at], late_sem
            ).start()

    def left_node(k, at):
        return graph[lax.rem(at, 2), graph[prod_left, k]]

    @pl.loop(0, half)
    def _(i):
        read_node(left_node(order[(1 - side) * half + i], i), left_cross.at[i], early_sem)
        read_node(left_node(order[side * half + i], i), left_own.at[i], early_sem)

    used[0] = 0
    used[1] = 0

    @pl.loop(0, count)
    def _(at):
        which = lax.div(at, half)
        right = graph[prod_right, order[at]]
        chip = chip_of[right]
        local = (chip >= 0) & (lax.div(jnp.maximum(chip, 0), groups // 2) == which)
        spare = jnp.minimum(used[which], extra - 1)
        flags[at] = graph[prod_flag, order[at]]
        left_slot[at] = jnp.where(local, lax.rem(jnp.maximum(chip, 0), groups // 2), 0)
        extra_slot[at] = jnp.where(local, 0, spare)
        is_extra[at] = jnp.where(local, 0, 1)
        extras[which * extra + spare] = jnp.where(
            local, extras[which * extra + spare], right
        )
        used[which] = used[which] + jnp.where(local, 0, 1)

    @pl.loop(0, extra)
    def _(e):
        pair = extras[(1 - side) * extra + e]
        read_node(graph[first_node, pair], a_cross.at[e], early_sem)
        read_chunks(graph[first_node + 1, pair], b_cross, e)

    @pl.loop(0, half)
    def _(i):
        right = graph[prod_right, order[side * half + i]]
        read_node(graph[first_node, right], a_own.at[i], early_sem)
        read_chunks(graph[first_node + 1, right], b_own, i)

    for h in range(2):
        base = h * slots

        @pl.loop(0, slots)
        def _(t):
            merges[2 * (base + t)] = half
            merges[2 * (base + t) + 1] = half

        def take(i, taken):
            diag = graph[prod_diag, order[h * half + i]]
            slot = slot_of[h * diags + diag]
            new = slot < 0
            slot = jnp.where(new, jnp.minimum(taken, slots - 1), slot)
            slot_of[h * diags + diag] = slot
            at = 2 * (base + slot)
            merges[at] = jnp.where(new, i, merges[at])
            merges[at + 1] = jnp.where(new, half, i)
            return taken + new.astype(jnp.int32)

        lax.fori_loop(0, half, take, jnp.int32(0))

    for h in range(2):

        @pl.loop(0, diags)
        def _(d):
            near = slot_of[h * diags + d]
            far = half + slot_of[(1 - h) * diags + d]
            here = near >= 0
            at = 2 * (h * slots + jnp.maximum(near, 0))
            both = here & (merges[at + 1] < half)
            finals[2 * (h * diags + d)] = jnp.where(here, merges[at], far)
            finals[2 * (h * diags + d) + 1] = jnp.where(
                both, merges[at + 1], jnp.where(here, far, half + slots)
            )

    for ref in (left_own, a_own, left_cross, a_cross):
        pltpu.make_async_copy(ref, ref, early_sem).wait()
    for ref in (b_own, b_cross):
        pltpu.make_async_copy(ref, ref, late_sem).wait()


def plan_and_gather(n, nodes, pair_nodes, prod_left, prod_right, prod_flag, prod_diag, chunks):
    count = prod_left.shape[0]
    _, parts, rows, order = nodes.shape
    half = groups = count // 2
    extra, slots = plan_sizes(count)
    width = order // chunks
    graph = jnp.stack(
        [pair_nodes[:, 0], pair_nodes[:, 1], prod_left, prod_right, prod_flag, prod_diag]
    )
    whole = lambda size: jax.ShapeDtypeStruct((size, parts, rows, order), nodes.dtype)
    cut = lambda size: jax.ShapeDtypeStruct((chunks, size, parts, rows, width), nodes.dtype)
    table = lambda size: jax.ShapeDtypeStruct((size,), jnp.int32)
    smem = pl.BlockSpec(memory_space=pltpu.SMEM)
    scratch = lambda size: pltpu.SMEM((size,), jnp.int32)
    return pl.pallas_call(
        functools.partial(plan_and_gather_kernel, n),
        out_shape=(
            table(count),
            table(count),
            table(count),
            table(count),
            table(4 * slots),
            table(4 * half),
            whole(half),
            whole(half),
            cut(half),
            whole(half),
            whole(extra),
            cut(extra),
        ),
        in_specs=[smem, pl.BlockSpec(memory_space=pltpu.HBM)],
        out_specs=[smem] * 6 + [pl.BlockSpec(memory_space=pltpu.VMEM)] * 6,
        scratch_shapes=[
            scratch(2 * count),
            scratch(count),
            scratch(2 * count),
            scratch(count),
            scratch(count),
            scratch(2 * extra),
            scratch(2),
            scratch(2 * half),
            scratch(count),
            pltpu.VMEM((groups, LANES), jnp.float32),
            pltpu.SemaphoreType.DMA,
            pltpu.SemaphoreType.DMA,
        ],
        compiler_params=pltpu.CompilerParams(vmem_limit_bytes=36 * 2**20),
    )(graph, nodes)


def tile_product(left_re, left_im, right_re, right_im):
    dot = functools.partial(jnp.dot, preferred_element_type=jnp.float32)
    real_part = dot(left_re, right_re) - dot(left_im, right_im)
    imag_part = dot(left_re, right_im) + dot(left_im, right_re)
    return real_part.astype(jnp.bfloat16), imag_part.astype(jnp.bfloat16)


def exchange_kernel(
    n,
    flags,
    left_slot,
    extra_slot,
    is_extra,
    merges,
    finals,
    left_own,
    a_own,
    b_own,
    left_cross,
    a_cross,
    b_cross,
    out,
    lefts,
    a_full,
    b_full,
    left_plain,
    right_pair,
    left_relay,
    a_relay,
    b_relay,
    b_pick,
    panels,
    relayed,
    merged,
    left_sem,
    a_sem,
    b_sem,
    swap_sem,
    left_relay_sem,
    a_relay_sem,
    b_relay_sem,
    near_sem,
    relay_sem,
    far_sem,
    left_out_sem,
    a_out_sem,
    b_out_sem,
    swap_out_sem,
    left_cross_sem,
    a_cross_sem,
    b_cross_sem,
    left_pick_sem,
    a_pick_sem,
    b_pick_sem,
    near_out_sem,
    relay_out_sem,
    far_out_sem,
):
    me = lax.axis_index("node")
    parity = lax.rem(me, 2)
    partner = me + 1 - 2 * parity
    chunks, _, order, width = b_full.shape
    rows = left_own.shape[2]
    half, quarter = n // 2, n // 4
    extra = a_relay[0].shape[0]
    bands = len(left_relay)
    band = rows // bands
    tiles = order // TILE
    side, place = lax.div(me, half), lax.rem(me, half)
    own, other = side * half, (1 - side) * half
    lane, hop = lax.rem(me, quarter), lax.div(place, quarter)
    relays = quarter + side * (half - quarter)
    to_relay = half - side * (half - quarter) + lane
    is_relay = hop + side == 1

    barrier = pltpu.get_barrier_semaphore()

    @pl.loop(1, n)
    def _(t):
        pl.semaphore_signal(
            barrier,
            inc=1,
            device_id={"node": lax.rem(me + t, n)},
            device_id_type=pl.DeviceIdType.MESH,
        )

    pl.semaphore_wait(barrier, n - 1)

    def push(src, dst, send_sem, recv_sem, to):
        pltpu.make_async_remote_copy(
            src_ref=src,
            dst_ref=dst,
            send_sem=send_sem,
            recv_sem=recv_sem,
            device_id={"node": to},
            device_id_type=pl.DeviceIdType.MESH,
        ).start()

    def keep(src, dst, sem):
        pltpu.make_async_copy(src, dst, sem).start()

    def landed(ref, sem):
        pltpu.make_async_copy(ref, ref, sem).wait()

    def rows_of(device):
        return pl.ds(pl.multiple_of(device * rows, rows), rows)

    def band_of(device, r):
        return pl.ds(pl.multiple_of(device * rows + r * band, band), band)

    my_rows = rows_of(me)
    near, far = pl.ds(0, half), pl.ds(half, merged.shape[2])
    owners = [other + lane, other + quarter + lane]

    def others(step):
        @pl.loop(1, half)
        def _(t):
            step(lax.rem(place + t, half))

    for r in range(bands):
        push(
            left_cross.at[:, :, pl.ds(r * band, band)],
            left_relay[r].at[:, hop],
            left_cross_sem,
            left_relay_sem.at[r],
            to_relay,
        )

    others(
        lambda i: push(
            left_own.at[i], lefts.at[lax.rem(i, 2), :, my_rows], left_out_sem, left_sem, own + i
        )
    )
    keep(left_own.at[place], lefts.at[parity, :, my_rows], left_sem)

    for r in range(bands):
        push(
            a_cross.at[:, :, pl.ds(r * band, band)],
            a_relay[r].at[:, hop],
            a_cross_sem,
            a_relay_sem.at[r],
            to_relay,
        )

    others(lambda i: push(a_own.at[i], a_full.at[:, my_rows], a_out_sem, a_sem, own + i))
    keep(a_own.at[place], a_full.at[:, my_rows], a_sem)

    def push_right(c):
        push(
            b_cross.at[c], b_relay[c].at[:, hop], b_cross_sem.at[c], b_relay_sem.at[c], to_relay
        )
        others(
            lambda i: push(
                b_own.at[c, i], b_full.at[c, :, my_rows], b_out_sem.at[c], b_sem.at[c], own + i
            )
        )
        keep(b_own.at[c, place], b_full.at[c, :, my_rows], b_sem.at[c])

    for c in range(min(AHEAD, chunks)):
        push_right(c)

    for c in range(chunks):
        panels[c][half + merged.shape[2]] = jnp.zeros(panels[c].shape[1:], panels[c].dtype)
        relayed[c][half] = jnp.zeros(relayed[c].shape[1:], relayed[c].dtype)

    @pl.when(is_relay)
    def _():
        for r in range(bands):
            landed(left_relay[r], left_relay_sem.at[r])
            for j, owner in enumerate(owners):
                others(
                    lambda i: push(
                        left_relay[r].at[i, j],
                        lefts.at[lax.rem(i, 2), :, band_of(owner, r)],
                        left_pick_sem,
                        left_sem,
                        own + i,
                    )
                )
                keep(left_relay[r].at[place, j], lefts.at[parity, :, band_of(owner, r)], left_sem)

    landed(lefts.at[parity], left_sem)
    push(lefts.at[parity], lefts.at[parity], swap_out_sem, swap_sem, partner)
    landed(lefts.at[1 - parity], swap_sem)

    def block(i):
        return pl.ds(pl.multiple_of(i * TILE, TILE), TILE)

    @pl.loop(0, tiles * tiles)
    def _(t):
        down, across = block(lax.div(t, tiles)), block(lax.rem(t, tiles))
        real_part, imag_part = tile_product(
            lefts[0, 0, down, :], lefts[0, 1, down, :], lefts[1, 0, :, across], lefts[1, 1, :, across]
        )
        left_plain[0, down, across] = real_part
        left_plain[1, down, across] = imag_part

    landed(lefts.at[parity], swap_out_sem)
    left_used = lefts.at[0]
    flipped = flags[me] == 1

    @pl.loop(0, tiles * tiles)
    def _(t):
        down, across = block(lax.div(t, tiles)), block(lax.rem(t, tiles))
        left_used[0, down, across] = jnp.where(
            flipped, left_plain[0, across, down].T, left_plain[0, down, across]
        )
        left_used[1, down, across] = jnp.where(
            flipped, -left_plain[1, across, down].T, left_plain[1, down, across]
        )

    def pick_rows(i, j, r):
        return pl.ds(pl.multiple_of((2 * i + j) * rows + r * band, band), band)

    @pl.when(is_relay)
    def _():
        for r in range(bands):
            landed(a_relay[r], a_relay_sem.at[r])

            @pl.loop(0, half)
            def _(i):
                known = left_relay[r][2 * left_slot[own + i]]
                new = a_relay[r][extra_slot[own + i]]
                value = jnp.where(is_extra[own + i] == 1, new, known)
                for j in range(2):
                    left_plain[:, pick_rows(i, j, r), :] = value[j]

            for j, owner in enumerate(owners):
                others(
                    lambda i: push(
                        left_plain.at[:, pick_rows(i, j, r)],
                        a_full.at[:, band_of(owner, r)],
                        a_pick_sem,
                        a_sem,
                        own + i,
                    )
                )
                keep(left_plain.at[:, pick_rows(place, j, r)], a_full.at[:, band_of(owner, r)], a_sem)

    landed(a_full, a_sem)

    def relay_right(c):
        landed(b_relay[c], b_relay_sem.at[c])

        @pl.loop(0, half)
        def _(i):
            for r in range(bands):
                known = left_relay[r][
                    2 * left_slot[own + i] + 1, :, :, :, c * width : (c + 1) * width
                ]
                new = b_relay[c][extra_slot[own + i], :, :, r * band : (r + 1) * band, :]
                value = jnp.where(is_extra[own + i] == 1, new, known)
                b_pick[c, i, :, :, r * band : (r + 1) * band, :] = value

        for j, owner in enumerate(owners):
            others(
                lambda i: push(
                    b_pick.at[c, i, j],
                    b_full.at[c, :, rows_of(owner)],
                    b_pick_sem.at[c],
                    b_sem.at[c],
                    own + i,
                )
            )
            keep(b_pick.at[c, place, j], b_full.at[c, :, rows_of(owner)], b_sem.at[c])

    def compute(c):
        landed(b_full.at[c], b_sem.at[c])

        @pl.loop(0, tiles)
        def _(i):
            down = block(i)
            real_part, imag_part = tile_product(
                a_full[0, down, :], a_full[1, down, :], b_full[c, 0], b_full[c, 1]
            )
            right_pair[0, down, :] = real_part
            right_pair[1, down, :] = imag_part

        @pl.loop(0, tiles)
        def _(i):
            down = block(i)
            real_part, imag_part = tile_product(
                left_used[0, down, :], left_used[1, down, :], right_pair[0], right_pair[1]
            )
            b_full[c, 0, down, :] = real_part
            b_full[c, 1, down, :] = imag_part

        def to_far(q):
            for j in range(2):
                push(
                    b_full.at[c, :, rows_of(other + j * quarter + q)],
                    relayed[c].at[place, j],
                    relay_out_sem.at[c],
                    relay_sem.at[c],
                    relays + q,
                )

        @pl.loop(1, quarter)
        def _(t):
            to_far(lax.rem(lane + t, quarter))

        @pl.when(is_relay)
        def _():
            for j, owner in enumerate(owners):
                keep(b_full.at[c, :, rows_of(owner)], relayed[c].at[place, j], relay_sem.at[c])

        @pl.when(jnp.logical_not(is_relay))
        def _():
            to_far(lane)

        others(
            lambda i: push(
                b_full.at[c, :, rows_of(own + i)],
                panels[c].at[place],
                near_out_sem.at[c],
                near_sem.at[c],
                own + i,
            )
        )
        keep(b_full.at[c, :, my_rows], panels[c].at[place], near_sem.at[c])

    def merge(c):
        landed(relayed[c].at[near], relay_sem.at[c])

        @pl.loop(0, merged.shape[2])
        def _(t):
            at = 2 * (side * merged.shape[2] + t)
            first = relayed[c][merges[at]].astype(jnp.float32)
            second = relayed[c][merges[at + 1]].astype(jnp.float32)
            total = (first + second).astype(merged.dtype)
            for j in range(2):
                merged[c, j, t] = total[j]

        for j, owner in enumerate(owners):
            push(merged.at[c, j], panels[c].at[far], far_out_sem.at[c], far_sem.at[c], owner)

    for c in range(chunks):
        pl.when(is_relay)(functools.partial(relay_right, c))
        compute(c)
        if c + AHEAD < chunks:
            push_right(c + AHEAD)
        pl.when(is_relay)(functools.partial(merge, c))

    for c in range(chunks):
        landed(panels[c].at[near], near_sem.at[c])
        landed(panels[c].at[far], far_sem.at[c])

        @pl.loop(0, out.shape[0])
        def _(d):
            at = 2 * (side * out.shape[0] + d)
            first = panels[c][finals[at]].astype(jnp.float32)
            second = panels[c][finals[at + 1]].astype(jnp.float32)
            out[d, :, :, c * width : (c + 1) * width] = (first + second).astype(out.dtype)

    rest = pl.ds(0, half - 1)
    landed(left_cross, left_cross_sem)
    landed(left_own.at[rest], left_out_sem)
    landed(a_cross, a_cross_sem)
    landed(a_own.at[rest], a_out_sem)
    for c in range(chunks):
        landed(b_cross.at[c], b_cross_sem.at[c])
        landed(b_own.at[c, rest], b_out_sem.at[c])
        landed(panels[c].at[rest], near_out_sem.at[c])
        landed(relayed[c].at[pl.ds(0, quarter - 1)], relay_out_sem.at[c])

    @pl.when(is_relay)
    def _():
        for r in range(bands):
            landed(left_relay[r].at[rest], left_pick_sem)
            landed(left_relay[r].at[rest], a_pick_sem)
        for c in range(chunks):
            landed(b_pick.at[c, rest], b_pick_sem.at[c])
            landed(merged.at[c], far_out_sem.at[c])

    @pl.when(jnp.logical_not(is_relay))
    def _():
        for c in range(chunks):
            landed(relayed[c].at[0], relay_out_sem.at[c])


def local(nodes, pair_nodes, prod_left, prod_right, prod_flag, prod_diag, *, n):
    _, parts, rows, order = nodes.shape
    count = prod_left.shape[0]
    assert count == n == pair_nodes.shape[0] and rows * n == order and n % 4 == 0
    half = diags = count // 2
    extra, slots = plan_sizes(count)
    chunks = order // WIDTH
    width = order // chunks
    bands = rows // BAND
    sources = 2
    tables_and_rows = plan_and_gather(
        n, nodes, pair_nodes, prod_left, prod_right, prod_flag, prod_diag, chunks
    )
    kind = nodes.dtype
    dma = pltpu.SemaphoreType.DMA
    smem = pl.BlockSpec(memory_space=pltpu.SMEM)
    anywhere = pl.BlockSpec(memory_space=pl.ANY)
    return pl.pallas_call(
        functools.partial(exchange_kernel, n),
        out_shape=jax.ShapeDtypeStruct((diags, parts, rows, order), kind),
        in_specs=[smem] * 6 + [anywhere] * 6,
        out_specs=pl.BlockSpec(memory_space=pltpu.VMEM),
        scratch_shapes=[
            pltpu.VMEM((2, parts, order, order), kind),
            pltpu.VMEM((parts, order, order), kind),
            pltpu.VMEM((chunks, parts, order, width), kind),
            pltpu.VMEM((parts, order, order), kind),
            pltpu.VMEM((parts, order, width), kind),
            [pltpu.VMEM((half, sources, parts, BAND, order), kind)] * bands,
            [pltpu.VMEM((extra, sources, parts, BAND, order), kind)] * bands,
            [pltpu.VMEM((extra, sources, parts, rows, width), kind)] * chunks,
            pltpu.VMEM((chunks, half, sources, parts, rows, width), kind),
            [pltpu.VMEM((half + slots + 1, parts, rows, width), kind)] * chunks,
            [pltpu.VMEM((half + 1, sources, parts, rows, width), kind)] * chunks,
            pltpu.VMEM((chunks, sources, slots, parts, rows, width), kind),
            dma,
            dma,
            dma((chunks,)),
            dma,
            dma((bands,)),
            dma((bands,)),
            dma((chunks,)),
            dma((chunks,)),
            dma((chunks,)),
            dma((chunks,)),
            dma,
            dma,
            dma((chunks,)),
            dma,
            dma,
            dma,
            dma((chunks,)),
            dma,
            dma,
            dma((chunks,)),
            dma((chunks,)),
            dma((chunks,)),
            dma((chunks,)),
        ],
        compiler_params=pltpu.CompilerParams(
            collective_id=0, has_side_effects=True, vmem_limit_bytes=51 * 2**20
        ),
    )(*tables_and_rows)


def solution(mesh):
    placed = (P("grp", None, "node", None), P(), P(), P(), P(), P())
    return jax.shard_map(
        functools.partial(local, n=mesh.shape["node"]),
        mesh=mesh,
        in_specs=placed,
        out_specs=P("grp", None, "node", None),
        check_vma=False,
    )
```

```python
import functools

import jax
import jax.numpy as jnp
from jax import lax
from jax.experimental import pallas as pl
from jax.experimental.pallas import tpu as pltpu
from jax.sharding import PartitionSpec as P

TILE = 256
WIDTH = 128
BAND = 16
LANES = 128


def searched(count):
    return 2 ** (count // 2 - 1) <= LANES


def plan_sizes(count):
    groups = count // 2
    if searched(count):
        return 3 * groups // 4, 3 * groups // 4
    return groups, groups


def choose_sides(graph, product, home, sides, group_of, extra, slots):
    groups = sides.shape[0]
    count = 2 * groups
    half = groups
    lane = lax.broadcasted_iota(jnp.int32, sides.shape, 1)
    group = lax.broadcasted_iota(jnp.int32, sides.shape, 0)
    sides[...] = lax.rem(lax.shift_right_logical(lane, group), 2).astype(jnp.float32)
    row = lambda g: sides[pl.ds(g, 1), :]
    zero = jnp.zeros((1, sides.shape[1]), jnp.float32)

    def add_group(g, carry):
        ones, inside_0, inside_1 = carry
        here = row(g)
        there = row(group_of[home[graph[2, product[2 * g]]]])
        return ones + here, inside_0 + (1 - here) * (1 - there), inside_1 + here * there

    ones, inside_0, inside_1 = lax.fori_loop(0, groups, add_group, (zero, zero, zero))

    def add_diag(k, carry):
        own_0, own_1 = carry
        k_mate = product[count + k]
        here, there = row(group_of[k]), row(group_of[k_mate])
        first = (k < k_mate).astype(jnp.float32)
        return own_0 + first * (1 - here * there), own_1 + first * jnp.maximum(here, there)

    own_0, own_1 = lax.fori_loop(0, count, add_diag, (zero, zero))
    new = half - jnp.minimum(inside_0, inside_1)
    own = jnp.maximum(own_0, own_1)
    bad = jnp.where(ones != groups // 2, 4096.0, 0.0)
    bad = bad + jnp.where(new > extra, 256.0, 0.0) + jnp.where(own > slots, 256.0, 0.0)
    cost = bad + 2 * new + own
    best = jnp.min(cost)
    index = lax.broadcasted_iota(jnp.int32, cost.shape, 1).astype(jnp.float32)
    return jnp.min(jnp.where(cost == best, index, 1e9)).astype(jnp.int32)


def plan_and_gather_kernel(
    n,
    graph,
    nodes,
    flags,
    left_slot,
    extra_slot,
    is_extra,
    merges,
    finals,
    left_own,
    a_own,
    b_own,
    left_cross,
    a_cross,
    b_cross,
    seen,
    group_of,
    product,
    home,
    chip_of,
    extras,
    used,
    slot_of,
    order,
    sides,
    early_sem,
    late_sem,
):
    count = graph.shape[1]
    groups = diags = half = count // 2
    extra = a_cross.shape[0]
    slots = merges.shape[0] // 4
    chunks = b_own.shape[0]
    width = b_own.shape[-1]
    first_node, prod_left, prod_right, prod_flag, prod_diag = 0, 2, 3, 4, 5
    me = lax.axis_index("node")
    side = lax.div(me, n // 2)

    @pl.loop(0, count)
    def _(p):
        seen[p] = -1
        seen[count + p] = -1
        chip_of[p] = -1

    @pl.loop(0, 2 * extra)
    def _(e):
        extras[e] = 0

    @pl.loop(0, 2 * diags)
    def _(d):
        slot_of[d] = -1

    def read(k, found):
        left = graph[prod_left, k]
        new = seen[left] < 0
        group = jnp.where(new, found, seen[left])
        seen[left] = group
        group_of[k] = group
        product[2 * group + 1] = k
        product[2 * group] = jnp.where(new, k, product[2 * group])
        home[graph[prod_right, k]] = k
        diag = graph[prod_diag, k]
        earlier = seen[count + diag]
        seen[count + diag] = k
        back = jnp.where(earlier < 0, k, earlier)
        product[count + k] = back
        product[count + back] = k
        return found + new.astype(jnp.int32)

    lax.fori_loop(0, count, read, jnp.int32(0))

    if not searched(count):
        mask = jnp.int32(2 ** (groups // 2) - 1)
    else:
        mask = choose_sides(graph, product, home, sides, group_of, extra, slots)

    def place(g, counts):
        which = lax.rem(lax.shift_right_logical(mask, g), 2)
        chip = jnp.where(which == 0, counts[0], groups // 2 + counts[1])
        order[2 * chip] = product[2 * g]
        order[2 * chip + 1] = product[2 * g + 1]
        chip_of[graph[prod_left, product[2 * g]]] = chip
        return counts[0] + 1 - which, counts[1] + which

    lax.fori_loop(0, groups, place, (jnp.int32(0), jnp.int32(0)))

    def read_node(node, dst, sem):
        pltpu.make_async_copy(nodes.at[node], dst, sem).start()

    def read_chunks(node, dst, at):
        for c in range(chunks):
            pltpu.make_async_copy(
                nodes.at[node, :, :, pl.ds(c * width, width)], dst.at[c, at], late_sem
            ).start()

    def left_node(k, at):
        return graph[lax.rem(at, 2), graph[prod_left, k]]

    @pl.loop(0, half)
    def _(i):
        read_node(left_node(order[(1 - side) * half + i], i), left_cross.at[i], early_sem)
        read_node(left_node(order[side * half + i], i), left_own.at[i], early_sem)

    used[0] = 0
    used[1] = 0

    @pl.loop(0, count)
    def _(at):
        which = lax.div(at, half)
        right = graph[prod_right, order[at]]
        chip = chip_of[right]
        local = (chip >= 0) & (lax.div(jnp.maximum(chip, 0), groups // 2) == which)
        spare = jnp.minimum(used[which], extra - 1)
        flags[at] = graph[prod_flag, order[at]]
        left_slot[at] = jnp.where(local, lax.rem(jnp.maximum(chip, 0), groups // 2), 0)
        extra_slot[at] = jnp.where(local, 0, spare)
        is_extra[at] = jnp.where(local, 0, 1)
        extras[which * extra + spare] = jnp.where(
            local, extras[which * extra + spare], right
        )
        used[which] = used[which] + jnp.where(local, 0, 1)

    @pl.loop(0, extra)
    def _(e):
        pair = extras[(1 - side) * extra + e]
        read_node(graph[first_node, pair], a_cross.at[e], early_sem)
        read_chunks(graph[first_node + 1, pair], b_cross, e)

    @pl.loop(0, half)
    def _(i):
        right = graph[prod_right, order[side * half + i]]
        read_node(graph[first_node, right], a_own.at[i], early_sem)
        read_chunks(graph[first_node + 1, right], b_own, i)

    for h in range(2):
        base = h * slots

        @pl.loop(0, slots)
        def _(t):
            merges[2 * (base + t)] = half
            merges[2 * (base + t) + 1] = half

        def take(i, taken):
            diag = graph[prod_diag, order[h * half + i]]
            slot = slot_of[h * diags + diag]
            new = slot < 0
            slot = jnp.where(new, jnp.minimum(taken, slots - 1), slot)
            slot_of[h * diags + diag] = slot
            at = 2 * (base + slot)
            merges[at] = jnp.where(new, i, merges[at])
            merges[at + 1] = jnp.where(new, half, i)
            return taken + new.astype(jnp.int32)

        lax.fori_loop(0, half, take, jnp.int32(0))

    for h in range(2):

        @pl.loop(0, diags)
        def _(d):
            near = slot_of[h * diags + d]
            far = half + slot_of[(1 - h) * diags + d]
            here = near >= 0
            at = 2 * (h * slots + jnp.maximum(near, 0))
            both = here & (merges[at + 1] < half)
            finals[2 * (h * diags + d)] = jnp.where(here, merges[at], far)
            finals[2 * (h * diags + d) + 1] = jnp.where(
                both, merges[at + 1], jnp.where(here, far, half + slots)
            )

    for ref in (left_own, a_own, left_cross, a_cross):
        pltpu.make_async_copy(ref, ref, early_sem).wait()
    for ref in (b_own, b_cross):
        pltpu.make_async_copy(ref, ref, late_sem).wait()


def plan_and_gather(n, nodes, pair_nodes, prod_left, prod_right, prod_flag, prod_diag, chunks):
    count = prod_left.shape[0]
    _, parts, rows, order = nodes.shape
    half = groups = count // 2
    extra, slots = plan_sizes(count)
    width = order // chunks
    graph = jnp.stack(
        [pair_nodes[:, 0], pair_nodes[:, 1], prod_left, prod_right, prod_flag, prod_diag]
    )
    whole = lambda size: jax.ShapeDtypeStruct((size, parts, rows, order), nodes.dtype)
    cut = lambda size: jax.ShapeDtypeStruct((chunks, size, parts, rows, width), nodes.dtype)
    table = lambda size: jax.ShapeDtypeStruct((size,), jnp.int32)
    smem = pl.BlockSpec(memory_space=pltpu.SMEM)
    scratch = lambda size: pltpu.SMEM((size,), jnp.int32)
    return pl.pallas_call(
        functools.partial(plan_and_gather_kernel, n),
        out_shape=(
            table(count),
            table(count),
            table(count),
            table(count),
            table(4 * slots),
            table(4 * half),
            whole(half),
            whole(half),
            cut(half),
            whole(half),
            whole(extra),
            cut(extra),
        ),
        in_specs=[smem, pl.BlockSpec(memory_space=pltpu.HBM)],
        out_specs=[smem] * 6 + [pl.BlockSpec(memory_space=pltpu.VMEM)] * 6,
        scratch_shapes=[
            scratch(2 * count),
            scratch(count),
            scratch(2 * count),
            scratch(count),
            scratch(count),
            scratch(2 * extra),
            scratch(2),
            scratch(2 * half),
            scratch(count),
            pltpu.VMEM((groups, LANES), jnp.float32),
            pltpu.SemaphoreType.DMA,
            pltpu.SemaphoreType.DMA,
        ],
        compiler_params=pltpu.CompilerParams(vmem_limit_bytes=36 * 2**20),
    )(graph, nodes)


def tile_product(left_re, left_im, right_re, right_im):
    dot = functools.partial(jnp.dot, preferred_element_type=jnp.float32)
    real_part = dot(left_re, right_re) - dot(left_im, right_im)
    imag_part = dot(left_re, right_im) + dot(left_im, right_re)
    return real_part.astype(jnp.bfloat16), imag_part.astype(jnp.bfloat16)


def exchange_kernel(
    n,
    flags,
    left_slot,
    extra_slot,
    is_extra,
    merges,
    finals,
    left_own,
    a_own,
    b_own,
    left_cross,
    a_cross,
    b_cross,
    out,
    lefts,
    a_full,
    b_full,
    left_plain,
    right_pair,
    left_relay,
    a_relay,
    b_relay,
    b_pick,
    panels,
    relayed,
    left_sem,
    a_sem,
    b_sem,
    swap_sem,
    left_relay_sem,
    a_relay_sem,
    b_relay_sem,
    near_sem,
    relay_sem,
    far_sem,
    left_out_sem,
    a_out_sem,
    b_out_sem,
    swap_out_sem,
    left_cross_sem,
    a_cross_sem,
    b_cross_sem,
    left_pick_sem,
    a_pick_sem,
    b_pick_sem,
    near_out_sem,
    relay_out_sem,
    far_out_sem,
):
    me = lax.axis_index("node")
    parity = lax.rem(me, 2)
    partner = me + 1 - 2 * parity
    chunks, _, order, width = b_full.shape
    rows = left_own.shape[2]
    half, quarter = n // 2, n // 4
    extra = a_relay[0][0].shape[0]
    bands = len(left_relay[0])
    band = rows // bands
    tiles = order // TILE
    side, place = lax.div(me, half), lax.rem(me, half)
    own, other = side * half, (1 - side) * half
    lane, hop = lax.rem(me, quarter), lax.div(place, quarter)
    relays = quarter + side * (half - quarter)
    to_relay = half - side * (half - quarter) + lane
    is_relay = hop + side == 1

    barrier = pltpu.get_barrier_semaphore()

    @pl.loop(1, n)
    def _(t):
        pl.semaphore_signal(
            barrier,
            inc=1,
            device_id={"node": lax.rem(me + t, n)},
            device_id_type=pl.DeviceIdType.MESH,
        )

    pl.semaphore_wait(barrier, n - 1)

    def push(src, dst, send_sem, recv_sem, to):
        pltpu.make_async_remote_copy(
            src_ref=src,
            dst_ref=dst,
            send_sem=send_sem,
            recv_sem=recv_sem,
            device_id={"node": to},
            device_id_type=pl.DeviceIdType.MESH,
        ).start()

    def keep(src, dst, sem):
        pltpu.make_async_copy(src, dst, sem).start()

    def landed(ref, sem):
        pltpu.make_async_copy(ref, ref, sem).wait()

    def rows_of(device):
        return pl.ds(pl.multiple_of(device * rows, rows), rows)

    def band_of(device, r):
        return pl.ds(pl.multiple_of(device * rows + r * band, band), band)

    my_rows = rows_of(me)
    slots = merges.shape[0] // 4
    near, far = pl.ds(0, half), pl.ds(half, slots)
    owners = [other + lane, other + quarter + lane]
    senders = [other + (1 - side) * quarter + lane, other + side * quarter + lane]

    def by_role(step):
        pl.when(jnp.logical_not(is_relay))(functools.partial(step, 0))
        pl.when(is_relay)(functools.partial(step, 1))

    def others(step):
        @pl.loop(1, half)
        def _(t):
            step(lax.rem(place + t, half))

    def cross_left(role):
        for r in range(bands):
            push(
                left_cross.at[:, :, pl.ds(r * band, band)],
                left_relay[role][r],
                left_cross_sem,
                left_relay_sem.at[role, r],
                to_relay,
            )

    def cross_a(role):
        for r in range(bands):
            push(
                a_cross.at[:, :, pl.ds(r * band, band)],
                a_relay[role][r],
                a_cross_sem,
                a_relay_sem.at[role, r],
                to_relay,
            )

    def cross_b(role):
        for c in range(chunks):
            push(
                b_cross.at[c],
                b_relay[c].at[pl.ds(0, extra), role],
                b_cross_sem.at[c],
                b_relay_sem.at[c],
                to_relay,
            )

    def share_b(c):
        others(
            lambda i: push(
                b_own.at[c, i], b_full.at[c, :, my_rows], b_out_sem.at[c], b_sem.at[c], own + i
            )
        )
        keep(b_own.at[c, place], b_full.at[c, :, my_rows], b_sem.at[c])

    def share_left():
        others(
            lambda i: push(
                left_own.at[i],
                lefts.at[lax.rem(i, 2), :, my_rows],
                left_out_sem,
                left_sem,
                own + i,
            )
        )
        keep(left_own.at[place], lefts.at[parity, :, my_rows], left_sem)

    def share_a():
        others(lambda i: push(a_own.at[i], a_full.at[:, my_rows], a_out_sem, a_sem, own + i))
        keep(a_own.at[place], a_full.at[:, my_rows], a_sem)

    by_role(cross_left)
    share_left()
    share_a()
    by_role(cross_a)

    @pl.when(jnp.logical_not(is_relay))
    def _():
        for c in range(chunks):
            share_b(c)

    pl.when(is_relay)(functools.partial(cross_b, 1))

    for c in range(chunks):
        panels[c][half + slots] = jnp.zeros(panels[c].shape[1:], panels[c].dtype)
        relayed[c][half] = jnp.zeros(relayed[c].shape[1:], relayed[c].dtype)

    @pl.when(is_relay)
    def _():
        for role, sender in enumerate(senders):
            for r in range(bands):
                landed(left_relay[role][r], left_relay_sem.at[role, r])
                others(
                    lambda i: push(
                        left_relay[role][r].at[i],
                        lefts.at[lax.rem(i, 2), :, band_of(sender, r)],
                        left_pick_sem,
                        left_sem,
                        own + i,
                    )
                )
                keep(
                    left_relay[role][r].at[place],
                    lefts.at[parity, :, band_of(sender, r)],
                    left_sem,
                )
        for c in range(chunks):
            share_b(c)

    landed(lefts.at[parity], left_sem)

    push(lefts.at[parity], lefts.at[parity], swap_out_sem, swap_sem, partner)
    landed(lefts.at[1 - parity], swap_sem)

    def block(i):
        return pl.ds(pl.multiple_of(i * TILE, TILE), TILE)

    @pl.loop(0, tiles * tiles)
    def _(t):
        down, across = block(lax.div(t, tiles)), block(lax.rem(t, tiles))
        real_part, imag_part = tile_product(
            lefts[0, 0, down, :], lefts[0, 1, down, :], lefts[1, 0, :, across], lefts[1, 1, :, across]
        )
        left_plain[0, down, across] = real_part
        left_plain[1, down, across] = imag_part

    landed(lefts.at[parity], swap_out_sem)
    left_used = lefts.at[0]
    flipped = flags[me] == 1

    @pl.loop(0, tiles * tiles)
    def _(t):
        down, across = block(lax.div(t, tiles)), block(lax.rem(t, tiles))
        left_used[0, down, across] = jnp.where(
            flipped, left_plain[0, across, down].T, left_plain[0, down, across]
        )
        left_used[1, down, across] = jnp.where(
            flipped, -left_plain[1, across, down].T, left_plain[1, down, across]
        )

    def pick_rows(i, role, r):
        return pl.ds(pl.multiple_of((2 * i + role) * rows + r * band, band), band)

    @pl.when(is_relay)
    def _():
        for role, sender in enumerate(senders):
            for r in range(bands):
                landed(a_relay[role][r], a_relay_sem.at[role, r])

                @pl.loop(0, half)
                def _(i):
                    known = left_relay[role][r][2 * left_slot[own + i]]
                    new = a_relay[role][r][extra_slot[own + i]]
                    left_plain[:, pick_rows(i, role, r), :] = jnp.where(
                        is_extra[own + i] == 1, new, known
                    )

                others(
                    lambda i: push(
                        left_plain.at[:, pick_rows(i, role, r)],
                        a_full.at[:, band_of(sender, r)],
                        a_pick_sem,
                        a_sem,
                        own + i,
                    )
                )
                keep(
                    left_plain.at[:, pick_rows(place, role, r)],
                    a_full.at[:, band_of(sender, r)],
                    a_sem,
                )

    landed(a_full, a_sem)
    pl.when(jnp.logical_not(is_relay))(functools.partial(cross_b, 0))

    def relay_right(c):
        landed(b_relay[c].at[pl.ds(0, extra)], b_relay_sem.at[c])
        across = pl.ds(c * width, width)

        @pl.loop(0, half)
        def _(i):
            for role in range(2):
                for r in range(bands):
                    down = pl.ds(r * band, band)
                    known = left_relay[role][r][2 * left_slot[own + i] + 1, :, :, across]
                    new = b_relay[c][extra_slot[own + i], role, :, down, :]
                    b_pick[c, i, role, :, down, :] = jnp.where(is_extra[own + i] == 1, new, known)

        for role, sender in enumerate(senders):
            others(
                lambda i: push(
                    b_pick.at[c, i, role],
                    b_full.at[c, :, rows_of(sender)],
                    b_pick_sem.at[c],
                    b_sem.at[c],
                    own + i,
                )
            )
            keep(b_pick.at[c, place, role], b_full.at[c, :, rows_of(sender)], b_sem.at[c])

    def compute(c):
        landed(b_full.at[c], b_sem.at[c])

        @pl.loop(0, tiles)
        def _(i):
            down = block(i)
            real_part, imag_part = tile_product(
                a_full[0, down, :], a_full[1, down, :], b_full[c, 0], b_full[c, 1]
            )
            right_pair[0, down, :] = real_part
            right_pair[1, down, :] = imag_part

        @pl.loop(0, tiles)
        def _(i):
            down = block(i)
            real_part, imag_part = tile_product(
                left_used[0, down, :], left_used[1, down, :], right_pair[0], right_pair[1]
            )
            b_full[c, 0, down, :] = real_part
            b_full[c, 1, down, :] = imag_part

        def to_far(q):
            for j in range(2):
                push(
                    b_full.at[c, :, rows_of(other + j * quarter + q)],
                    relayed[c].at[place, j],
                    relay_out_sem.at[c],
                    relay_sem.at[c],
                    relays + q,
                )

        @pl.loop(1, quarter)
        def _(t):
            to_far(lax.rem(lane + t, quarter))

        @pl.when(is_relay)
        def _():
            for j, owner in enumerate(owners):
                keep(b_full.at[c, :, rows_of(owner)], relayed[c].at[place, j], relay_sem.at[c])

        @pl.when(jnp.logical_not(is_relay))
        def _():
            to_far(lane)

        others(
            lambda i: push(
                b_full.at[c, :, rows_of(own + i)],
                panels[c].at[place],
                near_out_sem.at[c],
                near_sem.at[c],
                own + i,
            )
        )
        keep(b_full.at[c, :, my_rows], panels[c].at[place], near_sem.at[c])

    def merge(c):
        landed(relayed[c].at[near], relay_sem.at[c])

        @pl.loop(0, slots)
        def _(t):
            at = 2 * (side * slots + t)
            first = relayed[c][merges[at]].astype(jnp.float32)
            second = relayed[c][merges[at + 1]].astype(jnp.float32)
            b_relay[c][t] = (first + second).astype(out.dtype)

        for j, owner in enumerate(owners):
            push(
                b_relay[c].at[pl.ds(0, slots), j],
                panels[c].at[far],
                far_out_sem.at[c],
                far_sem.at[c],
                owner,
            )

    pl.when(is_relay)(functools.partial(relay_right, 0))
    for c in range(chunks):
        if c + 1 < chunks:
            pl.when(is_relay)(functools.partial(relay_right, c + 1))
        compute(c)
        if c > 0:
            pl.when(is_relay)(functools.partial(merge, c - 1))
    pl.when(is_relay)(functools.partial(merge, chunks - 1))

    for c in range(chunks):
        landed(panels[c].at[near], near_sem.at[c])
        landed(panels[c].at[far], far_sem.at[c])

        @pl.loop(0, out.shape[0])
        def _(d):
            at = 2 * (side * out.shape[0] + d)
            first = panels[c][finals[at]].astype(jnp.float32)
            second = panels[c][finals[at + 1]].astype(jnp.float32)
            out[d, :, :, c * width : (c + 1) * width] = (first + second).astype(out.dtype)

    rest = pl.ds(0, half - 1)
    landed(left_cross, left_cross_sem)
    landed(left_own.at[rest], left_out_sem)
    landed(a_cross, a_cross_sem)
    landed(a_own.at[rest], a_out_sem)
    for c in range(chunks):
        landed(b_cross.at[c], b_cross_sem.at[c])
        landed(b_own.at[c, rest], b_out_sem.at[c])
        landed(panels[c].at[rest], near_out_sem.at[c])
        landed(relayed[c].at[pl.ds(0, quarter - 1)], relay_out_sem.at[c])

    @pl.when(is_relay)
    def _():
        for role in range(2):
            for r in range(bands):
                landed(left_relay[role][r].at[rest], left_pick_sem)
                landed(left_relay[role][r].at[rest], a_pick_sem)
        for c in range(chunks):
            landed(b_pick.at[c, rest], b_pick_sem.at[c])
            landed(b_relay[c].at[pl.ds(0, slots)], far_out_sem.at[c])

    @pl.when(jnp.logical_not(is_relay))
    def _():
        for c in range(chunks):
            landed(relayed[c].at[0], relay_out_sem.at[c])


def local(nodes, pair_nodes, prod_left, prod_right, prod_flag, prod_diag, *, n):
    _, parts, rows, order = nodes.shape
    count = prod_left.shape[0]
    assert count == n == pair_nodes.shape[0] and rows * n == order and n % 4 == 0
    half = diags = count // 2
    extra, slots = plan_sizes(count)
    chunks = order // WIDTH
    width = order // chunks
    bands = rows // BAND
    sources = 2
    tables_and_rows = plan_and_gather(
        n, nodes, pair_nodes, prod_left, prod_right, prod_flag, prod_diag, chunks
    )
    kind = nodes.dtype
    matrix = parts * order * order
    blocks = 4 * half + 2 * extra + 2 * max(extra, slots) + (half + slots + 1) + 2 * (half + 1)
    held = 5 * matrix + parts * order * width + blocks * parts * rows * order
    dma = pltpu.SemaphoreType.DMA
    smem = pl.BlockSpec(memory_space=pltpu.SMEM)
    anywhere = pl.BlockSpec(memory_space=pl.ANY)
    return pl.pallas_call(
        functools.partial(exchange_kernel, n),
        out_shape=jax.ShapeDtypeStruct((diags, parts, rows, order), kind),
        in_specs=[smem] * 6 + [anywhere] * 6,
        out_specs=pl.BlockSpec(memory_space=pltpu.VMEM),
        scratch_shapes=[
            pltpu.VMEM((2, parts, order, order), kind),
            pltpu.VMEM((parts, order, order), kind),
            pltpu.VMEM((chunks, parts, order, width), kind),
            pltpu.VMEM((parts, order, order), kind),
            pltpu.VMEM((parts, order, width), kind),
            [[pltpu.VMEM((half, parts, BAND, order), kind)] * bands] * sources,
            [[pltpu.VMEM((extra, parts, BAND, order), kind)] * bands] * sources,
            [pltpu.VMEM((max(extra, slots), sources, parts, rows, width), kind)] * chunks,
            pltpu.VMEM((chunks, half, sources, parts, rows, width), kind),
            [pltpu.VMEM((half + slots + 1, parts, rows, width), kind)] * chunks,
            [pltpu.VMEM((half + 1, sources, parts, rows, width), kind)] * chunks,
            dma,
            dma,
            dma((chunks,)),
            dma,
            dma((sources, bands)),
            dma((sources, bands)),
            dma((chunks,)),
            dma((chunks,)),
            dma((chunks,)),
            dma((chunks,)),
            dma,
            dma,
            dma((chunks,)),
            dma,
            dma,
            dma,
            dma((chunks,)),
            dma,
            dma,
            dma((chunks,)),
            dma((chunks,)),
            dma((chunks,)),
            dma((chunks,)),
        ],
        compiler_params=pltpu.CompilerParams(
            collective_id=0, has_side_effects=True, vmem_limit_bytes=held * kind.itemsize + 2**20
        ),
    )(*tables_and_rows)


def solution(mesh):
    placed = (P("grp", None, "node", None), P(), P(), P(), P(), P())
    return jax.shard_map(
        functools.partial(local, n=mesh.shape["node"]),
        mesh=mesh,
        in_specs=placed,
        out_specs=P("grp", None, "node", None),
        check_vma=False,
    )
```

```python
import functools

import jax
import jax.numpy as jnp
from jax import lax
from jax.experimental import pallas as pl
from jax.experimental.pallas import tpu as pltpu
from jax.sharding import PartitionSpec as P

TILE = 256
WIDTH = 128
EARLY = 3
AHEAD = 3
BAND = 16
LANES = 128


def searched(count):
    return 2 ** (count // 2 - 1) <= LANES


def plan_sizes(count):
    groups = count // 2
    if searched(count):
        return 3 * groups // 4, 3 * groups // 4
    return groups, groups


def choose_sides(graph, product, home, sides, group_of, extra, slots):
    groups = sides.shape[0]
    count = 2 * groups
    half = groups
    lane = lax.broadcasted_iota(jnp.int32, sides.shape, 1)
    group = lax.broadcasted_iota(jnp.int32, sides.shape, 0)
    sides[...] = lax.rem(lax.shift_right_logical(lane, group), 2).astype(jnp.float32)
    row = lambda g: sides[pl.ds(g, 1), :]
    zero = jnp.zeros((1, sides.shape[1]), jnp.float32)

    def add_group(g, carry):
        ones, inside_0, inside_1 = carry
        here = row(g)
        there = row(group_of[home[graph[2, product[2 * g]]]])
        return ones + here, inside_0 + (1 - here) * (1 - there), inside_1 + here * there

    ones, inside_0, inside_1 = lax.fori_loop(0, groups, add_group, (zero, zero, zero))

    def add_diag(k, carry):
        own_0, own_1 = carry
        k_mate = product[count + k]
        here, there = row(group_of[k]), row(group_of[k_mate])
        first = (k < k_mate).astype(jnp.float32)
        return own_0 + first * (1 - here * there), own_1 + first * jnp.maximum(here, there)

    own_0, own_1 = lax.fori_loop(0, count, add_diag, (zero, zero))
    new = half - jnp.minimum(inside_0, inside_1)
    own = jnp.maximum(own_0, own_1)
    bad = jnp.where(ones != groups // 2, 4096.0, 0.0)
    bad = bad + jnp.where(new > extra, 256.0, 0.0) + jnp.where(own > slots, 256.0, 0.0)
    cost = bad + jnp.where(new > extra - 1, 64.0, 0.0) + 2 * new + own
    best = jnp.min(cost)
    index = lax.broadcasted_iota(jnp.int32, cost.shape, 1).astype(jnp.float32)
    mask = jnp.min(jnp.where(cost == best, index, 1e9)).astype(jnp.int32)
    return mask, (best < 64.0).astype(jnp.int32)


def plan_and_gather_kernel(
    n,
    graph,
    nodes,
    small,
    flags,
    left_slot,
    extra_slot,
    is_extra,
    merges,
    finals,
    left_own,
    a_own,
    b_own,
    left_cross,
    a_cross,
    b_cross,
    seen,
    group_of,
    product,
    home,
    chip_of,
    extras,
    used,
    slot_of,
    order,
    sides,
    early_sem,
    late_sem,
):
    count = graph.shape[1]
    groups = diags = half = count // 2
    extra = a_cross.shape[0]
    slots = merges.shape[0] // 4
    chunks = b_own.shape[0]
    width = b_own.shape[-1]
    first_node, prod_left, prod_right, prod_flag, prod_diag = 0, 2, 3, 4, 5
    me = lax.axis_index("node")
    side = lax.div(me, n // 2)

    @pl.loop(0, count)
    def _(p):
        seen[p] = -1
        seen[count + p] = -1
        chip_of[p] = -1

    @pl.loop(0, 2 * extra)
    def _(e):
        extras[e] = 0

    @pl.loop(0, 2 * diags)
    def _(d):
        slot_of[d] = -1

    def read(k, found):
        left = graph[prod_left, k]
        new = seen[left] < 0
        group = jnp.where(new, found, seen[left])
        seen[left] = group
        group_of[k] = group
        product[2 * group + 1] = k
        product[2 * group] = jnp.where(new, k, product[2 * group])
        home[graph[prod_right, k]] = k
        diag = graph[prod_diag, k]
        earlier = seen[count + diag]
        seen[count + diag] = k
        back = jnp.where(earlier < 0, k, earlier)
        product[count + k] = back
        product[count + back] = k
        return found + new.astype(jnp.int32)

    lax.fori_loop(0, count, read, jnp.int32(0))

    if not searched(count):
        mask, small[0] = jnp.int32(2 ** (groups // 2) - 1), 0
    else:
        mask, small[0] = choose_sides(graph, product, home, sides, group_of, extra, slots)

    def place(g, counts):
        which = lax.rem(lax.shift_right_logical(mask, g), 2)
        chip = jnp.where(which == 0, counts[0], groups // 2 + counts[1])
        order[2 * chip] = product[2 * g]
        order[2 * chip + 1] = product[2 * g + 1]
        chip_of[graph[prod_left, product[2 * g]]] = chip
        return counts[0] + 1 - which, counts[1] + which

    lax.fori_loop(0, groups, place, (jnp.int32(0), jnp.int32(0)))

    def read_node(node, dst, sem):
        pltpu.make_async_copy(nodes.at[node], dst, sem).start()

    def read_chunks(node, dst, at):
        for c in range(chunks):
            pltpu.make_async_copy(
                nodes.at[node, :, :, pl.ds(c * width, width)], dst.at[c, at], late_sem
            ).start()

    def left_node(k, at):
        return graph[lax.rem(at, 2), graph[prod_left, k]]

    @pl.loop(0, half)
    def _(i):
        read_node(left_node(order[(1 - side) * half + i], i), left_cross.at[i], early_sem)
        read_node(left_node(order[side * half + i], i), left_own.at[i], early_sem)

    used[0] = 0
    used[1] = 0

    @pl.loop(0, count)
    def _(at):
        which = lax.div(at, half)
        right = graph[prod_right, order[at]]
        chip = chip_of[right]
        local = (chip >= 0) & (lax.div(jnp.maximum(chip, 0), groups // 2) == which)
        spare = jnp.minimum(used[which], extra - 1)
        flags[at] = graph[prod_flag, order[at]]
        left_slot[at] = jnp.where(local, lax.rem(jnp.maximum(chip, 0), groups // 2), 0)
        extra_slot[at] = jnp.where(local, 0, spare)
        is_extra[at] = jnp.where(local, 0, 1)
        extras[which * extra + spare] = jnp.where(
            local, extras[which * extra + spare], right
        )
        used[which] = used[which] + jnp.where(local, 0, 1)

    @pl.loop(0, extra)
    def _(e):
        pair = extras[(1 - side) * extra + e]
        read_node(graph[first_node, pair], a_cross.at[e], early_sem)
        read_chunks(graph[first_node + 1, pair], b_cross, e)

    @pl.loop(0, half)
    def _(i):
        right = graph[prod_right, order[side * half + i]]
        read_node(graph[first_node, right], a_own.at[i], early_sem)
        read_chunks(graph[first_node + 1, right], b_own, i)

    for h in range(2):
        base = h * slots

        @pl.loop(0, slots)
        def _(t):
            merges[2 * (base + t)] = half
            merges[2 * (base + t) + 1] = half

        def take(i, taken):
            diag = graph[prod_diag, order[h * half + i]]
            slot = slot_of[h * diags + diag]
            new = slot < 0
            slot = jnp.where(new, jnp.minimum(taken, slots - 1), slot)
            slot_of[h * diags + diag] = slot
            at = 2 * (base + slot)
            merges[at] = jnp.where(new, i, merges[at])
            merges[at + 1] = jnp.where(new, half, i)
            return taken + new.astype(jnp.int32)

        lax.fori_loop(0, half, take, jnp.int32(0))

    for h in range(2):

        @pl.loop(0, diags)
        def _(d):
            near = slot_of[h * diags + d]
            far = half + slot_of[(1 - h) * diags + d]
            here = near >= 0
            at = 2 * (h * slots + jnp.maximum(near, 0))
            both = here & (merges[at + 1] < half)
            finals[2 * (h * diags + d)] = jnp.where(here, merges[at], far)
            finals[2 * (h * diags + d) + 1] = jnp.where(
                both, merges[at + 1], jnp.where(here, far, half + slots)
            )

    for ref in (left_own, a_own, left_cross, a_cross):
        pltpu.make_async_copy(ref, ref, early_sem).wait()
    for ref in (b_own, b_cross):
        pltpu.make_async_copy(ref, ref, late_sem).wait()


def plan_and_gather(n, nodes, pair_nodes, prod_left, prod_right, prod_flag, prod_diag, chunks):
    count = prod_left.shape[0]
    _, parts, rows, order = nodes.shape
    half = groups = count // 2
    extra, slots = plan_sizes(count)
    width = order // chunks
    graph = jnp.stack(
        [pair_nodes[:, 0], pair_nodes[:, 1], prod_left, prod_right, prod_flag, prod_diag]
    )
    whole = lambda size: jax.ShapeDtypeStruct((size, parts, rows, order), nodes.dtype)
    cut = lambda size: jax.ShapeDtypeStruct((chunks, size, parts, rows, width), nodes.dtype)
    table = lambda size: jax.ShapeDtypeStruct((size,), jnp.int32)
    smem = pl.BlockSpec(memory_space=pltpu.SMEM)
    scratch = lambda size: pltpu.SMEM((size,), jnp.int32)
    return pl.pallas_call(
        functools.partial(plan_and_gather_kernel, n),
        out_shape=(
            table(1),
            table(count),
            table(count),
            table(count),
            table(count),
            table(4 * slots),
            table(4 * half),
            whole(half),
            whole(half),
            cut(half),
            whole(half),
            whole(extra),
            cut(extra),
        ),
        in_specs=[smem, pl.BlockSpec(memory_space=pltpu.HBM)],
        out_specs=[smem] * 7 + [pl.BlockSpec(memory_space=pltpu.VMEM)] * 6,
        scratch_shapes=[
            scratch(2 * count),
            scratch(count),
            scratch(2 * count),
            scratch(count),
            scratch(count),
            scratch(2 * extra),
            scratch(2),
            scratch(2 * half),
            scratch(count),
            pltpu.VMEM((groups, LANES), jnp.float32),
            pltpu.SemaphoreType.DMA,
            pltpu.SemaphoreType.DMA,
        ],
        compiler_params=pltpu.CompilerParams(vmem_limit_bytes=50 * 2**20),
    )(graph, nodes)


def tile_product(left_re, left_im, right_re, right_im):
    dot = functools.partial(jnp.dot, preferred_element_type=jnp.float32)
    real_part = dot(left_re, right_re) - dot(left_im, right_im)
    imag_part = dot(left_re, right_im) + dot(left_im, right_re)
    return real_part.astype(jnp.bfloat16), imag_part.astype(jnp.bfloat16)


def exchange_kernel(
    n,
    flags,
    left_slot,
    extra_slot,
    is_extra,
    merges,
    finals,
    left_own,
    a_own,
    b_own,
    left_cross,
    a_cross,
    b_cross,
    out,
    lefts,
    a_full,
    b_full,
    left_plain,
    right_pair,
    left_relay,
    a_relay,
    b_relay,
    b_pick,
    panels,
    relayed,
    left_sem,
    a_sem,
    b_sem,
    swap_sem,
    left_relay_sem,
    a_relay_sem,
    b_relay_sem,
    near_sem,
    relay_sem,
    far_sem,
    left_out_sem,
    a_out_sem,
    b_out_sem,
    swap_out_sem,
    left_cross_sem,
    a_cross_sem,
    b_cross_sem,
    left_pick_sem,
    a_pick_sem,
    b_pick_sem,
    near_out_sem,
    relay_out_sem,
    far_out_sem,
):
    me = lax.axis_index("node")
    parity = lax.rem(me, 2)
    partner = me + 1 - 2 * parity
    chunks, _, order, width = b_full.shape
    rows = left_own.shape[2]
    half, quarter = n // 2, n // 4
    extra = a_relay[0][0].shape[0]
    bands = len(left_relay[0])
    band = rows // bands
    tiles = order // TILE
    side, place = lax.div(me, half), lax.rem(me, half)
    own, other = side * half, (1 - side) * half
    lane, hop = lax.rem(me, quarter), lax.div(place, quarter)
    relays = quarter + side * (half - quarter)
    to_relay = half - side * (half - quarter) + lane
    is_relay = hop + side == 1

    barrier = pltpu.get_barrier_semaphore()

    @pl.loop(1, n)
    def _(t):
        pl.semaphore_signal(
            barrier,
            inc=1,
            device_id={"node": lax.rem(me + t, n)},
            device_id_type=pl.DeviceIdType.MESH,
        )

    pl.semaphore_wait(barrier, n - 1)

    def push(src, dst, send_sem, recv_sem, to):
        pltpu.make_async_remote_copy(
            src_ref=src,
            dst_ref=dst,
            send_sem=send_sem,
            recv_sem=recv_sem,
            device_id={"node": to},
            device_id_type=pl.DeviceIdType.MESH,
        ).start()

    def keep(src, dst, sem):
        pltpu.make_async_copy(src, dst, sem).start()

    def landed(ref, sem):
        pltpu.make_async_copy(ref, ref, sem).wait()

    def rows_of(device):
        return pl.ds(pl.multiple_of(device * rows, rows), rows)

    def band_of(device, r):
        return pl.ds(pl.multiple_of(device * rows + r * band, band), band)

    my_rows = rows_of(me)
    slots = merges.shape[0] // 4
    near, far = pl.ds(0, half), pl.ds(half, slots)
    owners = [other + lane, other + quarter + lane]
    senders = [other + (1 - side) * quarter + lane, other + side * quarter + lane]

    def by_role(step):
        pl.when(jnp.logical_not(is_relay))(functools.partial(step, 0))
        pl.when(is_relay)(functools.partial(step, 1))

    def others(step):
        @pl.loop(1, half)
        def _(t):
            step(lax.rem(place + t, half))

    def cross_left(role):
        for r in range(bands):
            push(
                left_cross.at[:, :, pl.ds(r * band, band)],
                left_relay[role][r],
                left_cross_sem,
                left_relay_sem.at[role, r],
                to_relay,
            )

    def cross_a(role):
        for r in range(bands):
            push(
                a_cross.at[pl.ds(0, extra), :, pl.ds(r * band, band)],
                a_relay[role][r],
                a_cross_sem,
                a_relay_sem.at[role, r],
                to_relay,
            )

    def cross_b(role, c):
        push(
            b_cross.at[c, pl.ds(0, extra)],
            b_relay[role][c].at[pl.ds(0, extra)],
            b_cross_sem.at[c],
            b_relay_sem.at[role, c],
            to_relay,
        )

    def share_b(c):
        others(
            lambda i: push(
                b_own.at[c, i], b_full.at[c, :, my_rows], b_out_sem.at[c], b_sem.at[c], own + i
            )
        )
        keep(b_own.at[c, place], b_full.at[c, :, my_rows], b_sem.at[c])

    def share_left():
        others(
            lambda i: push(
                left_own.at[i],
                lefts.at[lax.rem(i, 2), :, my_rows],
                left_out_sem,
                left_sem,
                own + i,
            )
        )
        keep(left_own.at[place], lefts.at[parity, :, my_rows], left_sem)

    def share_a():
        others(
            lambda i: push(
                a_own.at[i], a_full.at[:, my_rows], a_out_sem, a_sem.at[2 * bands], own + i
            )
        )
        keep(a_own.at[place], a_full.at[:, my_rows], a_sem.at[2 * bands])

    by_role(cross_left)
    share_left()
    share_a()
    by_role(cross_a)

    @pl.when(jnp.logical_not(is_relay))
    def _():
        for c in range(chunks):
            share_b(c)

    for c in range(chunks):
        pl.when(is_relay)(functools.partial(cross_b, 1, c))

    for c in range(chunks):
        panels[c][half + slots] = jnp.zeros(panels[c].shape[1:], panels[c].dtype)
        relayed[c][half] = jnp.zeros(relayed[c].shape[1:], relayed[c].dtype)

    @pl.when(is_relay)
    def _():
        for role, sender in enumerate(senders):
            for r in range(bands):
                landed(left_relay[role][r], left_relay_sem.at[role, r])
                others(
                    lambda i: push(
                        left_relay[role][r].at[i],
                        lefts.at[lax.rem(i, 2), :, band_of(sender, r)],
                        left_pick_sem,
                        left_sem,
                        own + i,
                    )
                )
                keep(
                    left_relay[role][r].at[place],
                    lefts.at[parity, :, band_of(sender, r)],
                    left_sem,
                )
        for c in range(chunks):
            share_b(c)

    landed(lefts.at[parity], left_sem)

    push(lefts.at[parity], lefts.at[parity], swap_out_sem, swap_sem, partner)
    landed(lefts.at[1 - parity], swap_sem)

    def block(i):
        return pl.ds(pl.multiple_of(i * TILE, TILE), TILE)

    @pl.loop(0, tiles * tiles)
    def _(t):
        down, across = block(lax.div(t, tiles)), block(lax.rem(t, tiles))
        real_part, imag_part = tile_product(
            lefts[0, 0, down, :], lefts[0, 1, down, :], lefts[1, 0, :, across], lefts[1, 1, :, across]
        )
        left_plain[0, down, across] = real_part
        left_plain[1, down, across] = imag_part

    landed(lefts.at[parity], swap_out_sem)
    left_used = lefts.at[0]
    flipped = flags[me] == 1

    @pl.loop(0, tiles * tiles)
    def _(t):
        down, across = block(lax.div(t, tiles)), block(lax.rem(t, tiles))
        left_used[0, down, across] = jnp.where(
            flipped, left_plain[0, across, down].T, left_plain[0, down, across]
        )
        left_used[1, down, across] = jnp.where(
            flipped, -left_plain[1, across, down].T, left_plain[1, down, across]
        )

    def pick_rows(i, role, r):
        return pl.ds(pl.multiple_of((2 * i + role) * rows + r * band, band), band)

    @pl.when(is_relay)
    def _():
        for role, sender in enumerate(senders):
            for r in range(bands):
                landed(a_relay[role][r], a_relay_sem.at[role, r])

                @pl.loop(0, half)
                def _(i):
                    known = left_relay[role][r][2 * left_slot[own + i]]
                    new = a_relay[role][r][extra_slot[own + i]]
                    left_plain[:, pick_rows(i, role, r), :] = jnp.where(
                        is_extra[own + i] == 1, new, known
                    )

                others(
                    lambda i: push(
                        left_plain.at[:, pick_rows(i, role, r)],
                        a_full.at[:, band_of(sender, r)],
                        a_pick_sem,
                        a_sem.at[role * bands + r],
                        own + i,
                    )
                )
                keep(
                    left_plain.at[:, pick_rows(place, role, r)],
                    a_full.at[:, band_of(sender, r)],
                    a_sem.at[role * bands + r],
                )

    landed(a_full.at[:, pl.ds(0, quarter * band)], a_sem.at[max(2 * bands - 2, 0)])
    for c in range(min(AHEAD, chunks)):
        pl.when(jnp.logical_not(is_relay))(functools.partial(cross_b, 0, c))

    def relay_right(role, c):
        landed(b_relay[role][c].at[pl.ds(0, extra)], b_relay_sem.at[role, c])
        across = pl.ds(c * width, width)

        @pl.loop(0, half)
        def _(i):
            for r in range(bands):
                down = pl.ds(r * band, band)
                known = left_relay[role][r][2 * left_slot[own + i] + 1, :, :, across]
                new = b_relay[role][c][extra_slot[own + i], :, down, :]
                b_pick[c, i, role, :, down, :] = jnp.where(is_extra[own + i] == 1, new, known)

        others(
            lambda i: push(
                b_pick.at[c, i, role],
                b_full.at[c, :, rows_of(senders[role])],
                b_pick_sem.at[c],
                b_sem.at[c],
                own + i,
            )
        )
        keep(
            b_pick.at[c, place, role], b_full.at[c, :, rows_of(senders[role])], b_sem.at[c]
        )

    @pl.when(is_relay)
    def _():
        for c in range(min(EARLY, chunks)):
            relay_right(1, c)

    landed(a_full.at[:, pl.ds(0, half * rows)], a_sem.at[2 * bands])
    for t in range(2 * bands):
        if t != 2 * bands - 2:
            landed(a_full.at[:, pl.ds(0, quarter * band)], a_sem.at[t])

    def compute(c):
        @pl.loop(0, tiles)
        def _(i):
            down = block(i)
            real_part, imag_part = tile_product(
                a_full[0, down, :], a_full[1, down, :], b_full[c, 0], b_full[c, 1]
            )
            right_pair[0, down, :] = real_part
            right_pair[1, down, :] = imag_part

        def to_far(q):
            for j in range(2):
                push(
                    b_full.at[c, :, rows_of(other + j * quarter + q)],
                    relayed[c].at[place, j],
                    relay_out_sem.at[c],
                    relay_sem.at[c],
                    relays + q,
                )

        def all_far():
            @pl.loop(1, quarter)
            def _(t):
                to_far(lax.rem(lane + t, quarter))

            @pl.when(is_relay)
            def _():
                for j, owner in enumerate(owners):
                    keep(b_full.at[c, :, rows_of(owner)], relayed[c].at[place, j], relay_sem.at[c])

            @pl.when(jnp.logical_not(is_relay))
            def _():
                to_far(lane)

        piece = min(TILE, order // 2)

        @pl.loop(0, order // piece)
        def _(i):
            start = lax.rem(other * rows + i * piece, order)
            down = pl.ds(pl.multiple_of(start, piece), piece)
            real_part, imag_part = tile_product(
                left_used[0, down, :], left_used[1, down, :], right_pair[0], right_pair[1]
            )
            b_full[c, 0, down, :] = real_part
            b_full[c, 1, down, :] = imag_part
            pl.when(i == order // piece // 2 - 1)(all_far)

        others(
            lambda i: push(
                b_full.at[c, :, rows_of(own + i)],
                panels[c].at[place],
                near_out_sem.at[c],
                near_sem.at[c],
                own + i,
            )
        )
        keep(b_full.at[c, :, my_rows], panels[c].at[place], near_sem.at[c])

    def merge(c):
        landed(relayed[c].at[near], relay_sem.at[c])

        @pl.loop(0, slots)
        def _(t):
            at = 2 * (side * slots + t)
            first = relayed[c][merges[at]].astype(jnp.float32)
            second = relayed[c][merges[at + 1]].astype(jnp.float32)
            total = (first + second).astype(out.dtype)
            for j in range(2):
                b_relay[j][c][t] = total[j]

        for j, owner in enumerate(owners):
            push(
                b_relay[j][c].at[pl.ds(0, slots)],
                panels[c].at[far],
                far_out_sem.at[c],
                far_sem.at[c],
                owner,
            )

    pl.when(is_relay)(functools.partial(relay_right, 0, 0))
    for c in range(chunks):
        if c + 1 < chunks:
            pl.when(is_relay)(functools.partial(relay_right, 0, c + 1))
        if c + EARLY < chunks:
            pl.when(is_relay)(functools.partial(relay_right, 1, c + EARLY))
        landed(b_full.at[c], b_sem.at[c])
        if c + AHEAD < chunks:
            pl.when(jnp.logical_not(is_relay))(functools.partial(cross_b, 0, c + AHEAD))
        compute(c)
        if c > 0:
            pl.when(is_relay)(functools.partial(merge, c - 1))
    pl.when(is_relay)(functools.partial(merge, chunks - 1))

    for c in range(chunks):
        landed(panels[c].at[near], near_sem.at[c])
        landed(panels[c].at[far], far_sem.at[c])

        @pl.loop(0, out.shape[0])
        def _(d):
            at = 2 * (side * out.shape[0] + d)
            first = panels[c][finals[at]].astype(jnp.float32)
            second = panels[c][finals[at + 1]].astype(jnp.float32)
            out[d, :, :, c * width : (c + 1) * width] = (first + second).astype(out.dtype)

    rest = pl.ds(0, half - 1)
    landed(left_cross, left_cross_sem)
    landed(left_own.at[rest], left_out_sem)
    landed(a_cross.at[pl.ds(0, extra)], a_cross_sem)
    landed(a_own.at[rest], a_out_sem)
    for c in range(chunks):
        landed(b_cross.at[c, pl.ds(0, extra)], b_cross_sem.at[c])
        landed(b_own.at[c, rest], b_out_sem.at[c])
        landed(panels[c].at[rest], near_out_sem.at[c])
        landed(relayed[c].at[pl.ds(0, quarter - 1)], relay_out_sem.at[c])

    @pl.when(is_relay)
    def _():
        for role in range(2):
            for r in range(bands):
                landed(left_relay[role][r].at[rest], left_pick_sem)
                landed(left_relay[role][r].at[rest], a_pick_sem)
        for c in range(chunks):
            landed(b_pick.at[c, rest], b_pick_sem.at[c])
            for j in range(2):
                landed(b_relay[j][c].at[pl.ds(0, slots)], far_out_sem.at[c])

    @pl.when(jnp.logical_not(is_relay))
    def _():
        for c in range(chunks):
            landed(relayed[c].at[0], relay_out_sem.at[c])


def exchange(n, rows_in, extra, which):
    *_, merges, _, left_own, _, b_own, _, _, _ = rows_in
    half, parts, rows, order = left_own.shape
    chunks, width = b_own.shape[0], b_own.shape[-1]
    slots = merges.shape[0] // 4
    bands = rows // BAND
    sources = 2
    kind = left_own.dtype
    matrix = parts * order * order
    blocks = 4 * half + 2 * extra + 2 * max(extra, slots) + (half + slots + 1) + 2 * (half + 1)
    held = 5 * matrix + parts * order * width + blocks * parts * rows * order
    dma = pltpu.SemaphoreType.DMA
    smem = pl.BlockSpec(memory_space=pltpu.SMEM)
    anywhere = pl.BlockSpec(memory_space=pl.ANY)
    return pl.pallas_call(
        functools.partial(exchange_kernel, n),
        out_shape=jax.ShapeDtypeStruct((half, parts, rows, order), kind),
        in_specs=[smem] * 6 + [anywhere] * 6,
        out_specs=pl.BlockSpec(memory_space=pltpu.VMEM),
        scratch_shapes=[
            pltpu.VMEM((2, parts, order, order), kind),
            pltpu.VMEM((parts, order, order), kind),
            pltpu.VMEM((chunks, parts, order, width), kind),
            pltpu.VMEM((parts, order, order), kind),
            pltpu.VMEM((parts, order, width), kind),
            [[pltpu.VMEM((half, parts, BAND, order), kind)] * bands] * sources,
            [[pltpu.VMEM((extra, parts, BAND, order), kind)] * bands] * sources,
            [[pltpu.VMEM((max(extra, slots), parts, rows, width), kind)] * chunks] * sources,
            pltpu.VMEM((chunks, half, sources, parts, rows, width), kind),
            [pltpu.VMEM((half + slots + 1, parts, rows, width), kind)] * chunks,
            [pltpu.VMEM((half + 1, sources, parts, rows, width), kind)] * chunks,
            dma,
            dma((2 * bands + 1,)),
            dma((chunks,)),
            dma,
            dma((sources, bands)),
            dma((sources, bands)),
            dma((sources, chunks)),
            dma((chunks,)),
            dma((chunks,)),
            dma((chunks,)),
            dma,
            dma,
            dma((chunks,)),
            dma,
            dma,
            dma,
            dma((chunks,)),
            dma,
            dma,
            dma((chunks,)),
            dma((chunks,)),
            dma((chunks,)),
            dma((chunks,)),
        ],
        compiler_params=pltpu.CompilerParams(
            collective_id=which,
            has_side_effects=True,
            vmem_limit_bytes=held * kind.itemsize + 2**20,
        ),
    )(*rows_in)


def local(nodes, pair_nodes, prod_left, prod_right, prod_flag, prod_diag, *, n):
    _, parts, rows, order = nodes.shape
    count = prod_left.shape[0]
    assert count == n == pair_nodes.shape[0] and rows * n == order and n % 4 == 0
    extra, _ = plan_sizes(count)
    small, *rows_in = plan_and_gather(
        n, nodes, pair_nodes, prod_left, prod_right, prod_flag, prod_diag, order // WIDTH
    )
    whole = lambda *rows_in: exchange(n, rows_in, extra, 0)
    if not searched(count):
        return whole(*rows_in)
    return lax.cond(
        small[0] == 1, lambda *rows_in: exchange(n, rows_in, extra - 1, 1), whole, *rows_in
    )


def solution(mesh):
    placed = (P("grp", None, "node", None), P(), P(), P(), P(), P())
    return jax.shard_map(
        functools.partial(local, n=mesh.shape["node"]),
        mesh=mesh,
        in_specs=placed,
        out_specs=P("grp", None, "node", None),
        check_vma=False,
    )
```

```python
import functools

import jax
import jax.numpy as jnp
from jax import lax
from jax.experimental import pallas as pl
from jax.experimental.pallas import tpu as pltpu
from jax.sharding import PartitionSpec as P

TILE = 256
WIDTH = 128
EARLY = 3
AHEAD = 3
BAND = 16
LANES = 128


def searched(count):
    return 2 ** (count // 2 - 1) <= LANES


def plan_sizes(count):
    groups = count // 2
    if not searched(count):
        return [(groups, groups)]
    extra = slots = 3 * groups // 4
    return [(extra - 1, slots - 1), (extra - 1, slots), (extra, slots)]


def choose_sides(graph, product, home, sides, group_of):
    groups = sides.shape[0]
    count = 2 * groups
    half = groups
    lane = lax.broadcasted_iota(jnp.int32, sides.shape, 1)
    group = lax.broadcasted_iota(jnp.int32, sides.shape, 0)
    sides[...] = lax.rem(lax.shift_right_logical(lane, group), 2).astype(jnp.float32)
    row = lambda g: sides[pl.ds(g, 1), :]
    zero = jnp.zeros((1, sides.shape[1]), jnp.float32)

    def add_group(g, carry):
        ones, inside_0, inside_1 = carry
        here = row(g)
        there = row(group_of[home[graph[2, product[2 * g]]]])
        return ones + here, inside_0 + (1 - here) * (1 - there), inside_1 + here * there

    ones, inside_0, inside_1 = lax.fori_loop(0, groups, add_group, (zero, zero, zero))

    def add_diag(k, carry):
        own_0, own_1 = carry
        k_mate = product[count + k]
        here, there = row(group_of[k]), row(group_of[k_mate])
        first = (k < k_mate).astype(jnp.float32)
        return own_0 + first * (1 - here * there), own_1 + first * jnp.maximum(here, there)

    own_0, own_1 = lax.fori_loop(0, count, add_diag, (zero, zero))
    new = half - jnp.minimum(inside_0, inside_1)
    own = jnp.maximum(own_0, own_1)
    cost = jnp.full(new.shape, 64.0)
    sizes = plan_sizes(count)
    for index in reversed(range(len(sizes))):
        fits = (new <= sizes[index][0]) & (own <= sizes[index][1]) & (ones == groups // 2)
        cost = jnp.where(fits, float(index), cost)
    best = jnp.min(cost)
    index = lax.broadcasted_iota(jnp.int32, cost.shape, 1).astype(jnp.float32)
    mask = jnp.min(jnp.where(cost == best, index, 1e9)).astype(jnp.int32)
    return mask, jnp.minimum(best, float(len(sizes) - 1)).astype(jnp.int32)


def plan_and_gather_kernel(
    n,
    graph,
    nodes,
    kind_of,
    flags,
    left_slot,
    extra_slot,
    is_extra,
    merges,
    finals,
    left_own,
    a_own,
    b_own,
    left_cross,
    a_cross,
    b_cross,
    seen,
    group_of,
    product,
    home,
    chip_of,
    extras,
    used,
    slot_of,
    order,
    sides,
    early_sem,
    late_sem,
):
    count = graph.shape[1]
    groups = diags = half = count // 2
    extra = a_cross.shape[0]
    slots = merges.shape[0] // 4
    chunks = b_own.shape[0]
    width = b_own.shape[-1]
    first_node, prod_left, prod_right, prod_flag, prod_diag = 0, 2, 3, 4, 5
    me = lax.axis_index("node")
    side = lax.div(me, n // 2)

    @pl.loop(0, count)
    def _(p):
        seen[p] = -1
        seen[count + p] = -1
        chip_of[p] = -1

    @pl.loop(0, 2 * extra)
    def _(e):
        extras[e] = 0

    @pl.loop(0, 2 * diags)
    def _(d):
        slot_of[d] = -1

    def read(k, found):
        left = graph[prod_left, k]
        new = seen[left] < 0
        group = jnp.where(new, found, seen[left])
        seen[left] = group
        group_of[k] = group
        product[2 * group + 1] = k
        product[2 * group] = jnp.where(new, k, product[2 * group])
        home[graph[prod_right, k]] = k
        diag = graph[prod_diag, k]
        earlier = seen[count + diag]
        seen[count + diag] = k
        back = jnp.where(earlier < 0, k, earlier)
        product[count + k] = back
        product[count + back] = k
        return found + new.astype(jnp.int32)

    lax.fori_loop(0, count, read, jnp.int32(0))

    if not searched(count):
        mask, kind_of[0] = jnp.int32(2 ** (groups // 2) - 1), 0
    else:
        mask, kind_of[0] = choose_sides(graph, product, home, sides, group_of)

    def place(g, counts):
        which = lax.rem(lax.shift_right_logical(mask, g), 2)
        chip = jnp.where(which == 0, counts[0], groups // 2 + counts[1])
        order[2 * chip] = product[2 * g]
        order[2 * chip + 1] = product[2 * g + 1]
        chip_of[graph[prod_left, product[2 * g]]] = chip
        return counts[0] + 1 - which, counts[1] + which

    lax.fori_loop(0, groups, place, (jnp.int32(0), jnp.int32(0)))

    def read_node(node, dst, sem):
        pltpu.make_async_copy(nodes.at[node], dst, sem).start()

    def read_chunks(node, dst, at):
        for c in range(chunks):
            pltpu.make_async_copy(
                nodes.at[node, :, :, pl.ds(c * width, width)], dst.at[c, at], late_sem
            ).start()

    def left_node(k, at):
        return graph[lax.rem(at, 2), graph[prod_left, k]]

    @pl.loop(0, half)
    def _(i):
        read_node(left_node(order[(1 - side) * half + i], i), left_cross.at[i], early_sem)
        read_node(left_node(order[side * half + i], i), left_own.at[i], early_sem)

    used[0] = 0
    used[1] = 0

    @pl.loop(0, count)
    def _(at):
        which = lax.div(at, half)
        right = graph[prod_right, order[at]]
        chip = chip_of[right]
        local = (chip >= 0) & (lax.div(jnp.maximum(chip, 0), groups // 2) == which)
        spare = jnp.minimum(used[which], extra - 1)
        flags[at] = graph[prod_flag, order[at]]
        left_slot[at] = jnp.where(local, lax.rem(jnp.maximum(chip, 0), groups // 2), 0)
        extra_slot[at] = jnp.where(local, 0, spare)
        is_extra[at] = jnp.where(local, 0, 1)
        extras[which * extra + spare] = jnp.where(
            local, extras[which * extra + spare], right
        )
        used[which] = used[which] + jnp.where(local, 0, 1)

    @pl.loop(0, extra)
    def _(e):
        pair = extras[(1 - side) * extra + e]
        read_node(graph[first_node, pair], a_cross.at[e], early_sem)
        read_chunks(graph[first_node + 1, pair], b_cross, e)

    @pl.loop(0, half)
    def _(i):
        right = graph[prod_right, order[side * half + i]]
        read_node(graph[first_node, right], a_own.at[i], early_sem)
        read_chunks(graph[first_node + 1, right], b_own, i)

    for h in range(2):
        base = h * slots

        @pl.loop(0, slots)
        def _(t):
            merges[2 * (base + t)] = half
            merges[2 * (base + t) + 1] = half

        def take(i, taken):
            diag = graph[prod_diag, order[h * half + i]]
            slot = slot_of[h * diags + diag]
            new = slot < 0
            slot = jnp.where(new, jnp.minimum(taken, slots - 1), slot)
            slot_of[h * diags + diag] = slot
            at = 2 * (base + slot)
            merges[at] = jnp.where(new, i, merges[at])
            merges[at + 1] = jnp.where(new, half, i)
            return taken + new.astype(jnp.int32)

        lax.fori_loop(0, half, take, jnp.int32(0))

    for h in range(2):

        @pl.loop(0, diags)
        def _(d):
            near = slot_of[h * diags + d]
            far = half + slot_of[(1 - h) * diags + d]
            here = near >= 0
            at = 2 * (h * slots + jnp.maximum(near, 0))
            both = here & (merges[at + 1] < half)
            finals[2 * (h * diags + d)] = jnp.where(here, merges[at], far)
            finals[2 * (h * diags + d) + 1] = jnp.where(
                both, merges[at + 1], jnp.where(here, far, half + slots)
            )

    for ref in (left_own, a_own, left_cross, a_cross):
        pltpu.make_async_copy(ref, ref, early_sem).wait()
    for ref in (b_own, b_cross):
        pltpu.make_async_copy(ref, ref, late_sem).wait()


def plan_and_gather(n, nodes, pair_nodes, prod_left, prod_right, prod_flag, prod_diag, chunks):
    count = prod_left.shape[0]
    _, parts, rows, order = nodes.shape
    half = groups = count // 2
    extra, slots = plan_sizes(count)[-1]
    width = order // chunks
    graph = jnp.stack(
        [pair_nodes[:, 0], pair_nodes[:, 1], prod_left, prod_right, prod_flag, prod_diag]
    )
    whole = lambda size: jax.ShapeDtypeStruct((size, parts, rows, order), nodes.dtype)
    cut = lambda size: jax.ShapeDtypeStruct((chunks, size, parts, rows, width), nodes.dtype)
    table = lambda size: jax.ShapeDtypeStruct((size,), jnp.int32)
    smem = pl.BlockSpec(memory_space=pltpu.SMEM)
    scratch = lambda size: pltpu.SMEM((size,), jnp.int32)
    return pl.pallas_call(
        functools.partial(plan_and_gather_kernel, n),
        out_shape=(
            table(1),
            table(count),
            table(count),
            table(count),
            table(count),
            table(4 * slots),
            table(4 * half),
            whole(half),
            whole(half),
            cut(half),
            whole(half),
            whole(extra),
            cut(extra),
        ),
        in_specs=[smem, pl.BlockSpec(memory_space=pltpu.HBM)],
        out_specs=[smem] * 7 + [pl.BlockSpec(memory_space=pltpu.VMEM)] * 6,
        scratch_shapes=[
            scratch(2 * count),
            scratch(count),
            scratch(2 * count),
            scratch(count),
            scratch(count),
            scratch(2 * extra),
            scratch(2),
            scratch(2 * half),
            scratch(count),
            pltpu.VMEM((groups, LANES), jnp.float32),
            pltpu.SemaphoreType.DMA,
            pltpu.SemaphoreType.DMA,
        ],
        compiler_params=pltpu.CompilerParams(vmem_limit_bytes=50 * 2**20),
    )(graph, nodes)


def tile_product(left_re, left_im, right_re, right_im):
    dot = functools.partial(jnp.dot, preferred_element_type=jnp.float32)
    real_part = dot(left_re, right_re) - dot(left_im, right_im)
    imag_part = dot(left_re, right_im) + dot(left_im, right_re)
    return real_part.astype(jnp.bfloat16), imag_part.astype(jnp.bfloat16)


def exchange_kernel(
    n,
    slots,
    flags,
    left_slot,
    extra_slot,
    is_extra,
    merges,
    finals,
    left_own,
    a_own,
    b_own,
    left_cross,
    a_cross,
    b_cross,
    out,
    lefts,
    a_full,
    b_full,
    left_plain,
    right_pair,
    left_relay,
    a_relay,
    b_relay,
    b_pick,
    panels,
    relayed,
    left_sem,
    a_sem,
    b_sem,
    swap_sem,
    left_relay_sem,
    a_relay_sem,
    b_relay_sem,
    near_sem,
    relay_sem,
    far_sem,
    left_out_sem,
    a_out_sem,
    b_out_sem,
    swap_out_sem,
    left_cross_sem,
    a_cross_sem,
    b_cross_sem,
    left_pick_sem,
    a_pick_sem,
    b_pick_sem,
    near_out_sem,
    relay_out_sem,
    far_out_sem,
):
    me = lax.axis_index("node")
    parity = lax.rem(me, 2)
    partner = me + 1 - 2 * parity
    chunks, _, order, width = b_full.shape
    rows = left_own.shape[2]
    half, quarter = n // 2, n // 4
    extra = a_relay[0][0].shape[0]
    bands = len(left_relay[0])
    band = rows // bands
    tiles = order // TILE
    side, place = lax.div(me, half), lax.rem(me, half)
    own, other = side * half, (1 - side) * half
    lane, hop = lax.rem(me, quarter), lax.div(place, quarter)
    relays = quarter + side * (half - quarter)
    to_relay = half - side * (half - quarter) + lane
    is_relay = hop + side == 1

    barrier = pltpu.get_barrier_semaphore()

    def greet(device):
        pl.semaphore_signal(
            barrier, inc=1, device_id={"node": device}, device_id_type=pl.DeviceIdType.MESH
        )

    @pl.loop(1, half)
    def _(t):
        greet(own + lax.rem(place + t, half))

    greet(to_relay)

    @pl.when(is_relay)
    def _():
        greet(other + (1 - side) * quarter + lane)

    pl.semaphore_wait(barrier, half + jnp.where(is_relay, 1, 0))

    def push(src, dst, send_sem, recv_sem, to):
        pltpu.make_async_remote_copy(
            src_ref=src,
            dst_ref=dst,
            send_sem=send_sem,
            recv_sem=recv_sem,
            device_id={"node": to},
            device_id_type=pl.DeviceIdType.MESH,
        ).start()

    def keep(src, dst, sem):
        pltpu.make_async_copy(src, dst, sem).start()

    def landed(ref, sem):
        pltpu.make_async_copy(ref, ref, sem).wait()

    def rows_of(device):
        return pl.ds(pl.multiple_of(device * rows, rows), rows)

    def band_of(device, r):
        return pl.ds(pl.multiple_of(device * rows + r * band, band), band)

    my_rows = rows_of(me)
    most = merges.shape[0] // 4
    near, far = pl.ds(0, half), pl.ds(half, slots)
    owners = [other + lane, other + quarter + lane]
    senders = [other + (1 - side) * quarter + lane, other + side * quarter + lane]

    def by_role(step):
        pl.when(jnp.logical_not(is_relay))(functools.partial(step, 0))
        pl.when(is_relay)(functools.partial(step, 1))

    def others(step):
        @pl.loop(1, half)
        def _(t):
            step(lax.rem(place + t, half))

    def cross_left(role):
        for r in range(bands):
            push(
                left_cross.at[:, :, pl.ds(r * band, band)],
                left_relay[role][r],
                left_cross_sem,
                left_relay_sem.at[role, r],
                to_relay,
            )

    def cross_a(role):
        for r in range(bands):
            push(
                a_cross.at[pl.ds(0, extra), :, pl.ds(r * band, band)],
                a_relay[role][r],
                a_cross_sem,
                a_relay_sem.at[role, r],
                to_relay,
            )

    def cross_b(role, c):
        push(
            b_cross.at[c, pl.ds(0, extra)],
            b_relay[role][c].at[pl.ds(0, extra)],
            b_cross_sem.at[c],
            b_relay_sem.at[role, c],
            to_relay,
        )

    def share_b(c):
        others(
            lambda i: push(
                b_own.at[c, i], b_full.at[c, :, my_rows], b_out_sem.at[c], b_sem.at[c], own + i
            )
        )
        keep(b_own.at[c, place], b_full.at[c, :, my_rows], b_sem.at[c])

    def share_left():
        others(
            lambda i: push(
                left_own.at[i],
                lefts.at[lax.rem(i, 2), :, my_rows],
                left_out_sem,
                left_sem,
                own + i,
            )
        )
        keep(left_own.at[place], lefts.at[parity, :, my_rows], left_sem)

    def share_a():
        others(
            lambda i: push(
                a_own.at[i], a_full.at[:, my_rows], a_out_sem, a_sem.at[2 * bands], own + i
            )
        )
        keep(a_own.at[place], a_full.at[:, my_rows], a_sem.at[2 * bands])

    by_role(cross_left)
    share_left()
    share_a()
    by_role(cross_a)

    @pl.when(jnp.logical_not(is_relay))
    def _():
        for c in range(chunks):
            share_b(c)

    for c in range(chunks):
        pl.when(is_relay)(functools.partial(cross_b, 1, c))

    for c in range(chunks):
        for unused in range(slots, most + 1):
            panels[c][half + unused] = jnp.zeros(panels[c].shape[1:], panels[c].dtype)
        relayed[c][half] = jnp.zeros(relayed[c].shape[1:], relayed[c].dtype)

    @pl.when(is_relay)
    def _():
        for role, sender in enumerate(senders):
            for r in range(bands):
                landed(left_relay[role][r], left_relay_sem.at[role, r])
                others(
                    lambda i: push(
                        left_relay[role][r].at[i],
                        lefts.at[lax.rem(i, 2), :, band_of(sender, r)],
                        left_pick_sem,
                        left_sem,
                        own + i,
                    )
                )
                keep(
                    left_relay[role][r].at[place],
                    lefts.at[parity, :, band_of(sender, r)],
                    left_sem,
                )
        for c in range(chunks):
            share_b(c)

    landed(lefts.at[parity], left_sem)

    push(lefts.at[parity], lefts.at[parity], swap_out_sem, swap_sem, partner)
    landed(lefts.at[1 - parity], swap_sem)

    def block(i):
        return pl.ds(pl.multiple_of(i * TILE, TILE), TILE)

    @pl.loop(0, tiles * tiles)
    def _(t):
        down, across = block(lax.div(t, tiles)), block(lax.rem(t, tiles))
        real_part, imag_part = tile_product(
            lefts[0, 0, down, :], lefts[0, 1, down, :], lefts[1, 0, :, across], lefts[1, 1, :, across]
        )
        left_plain[0, down, across] = real_part
        left_plain[1, down, across] = imag_part

    landed(lefts.at[parity], swap_out_sem)
    left_used = lefts.at[0]
    flipped = flags[me] == 1

    @pl.loop(0, tiles * tiles)
    def _(t):
        down, across = block(lax.div(t, tiles)), block(lax.rem(t, tiles))
        left_used[0, down, across] = jnp.where(
            flipped, left_plain[0, across, down].T, left_plain[0, down, across]
        )
        left_used[1, down, across] = jnp.where(
            flipped, -left_plain[1, across, down].T, left_plain[1, down, across]
        )

    def pick_rows(i, role, r):
        return pl.ds(pl.multiple_of((2 * i + role) * rows + r * band, band), band)

    @pl.when(is_relay)
    def _():
        for role, sender in enumerate(senders):
            for r in range(bands):
                landed(a_relay[role][r], a_relay_sem.at[role, r])

                @pl.loop(0, half)
                def _(i):
                    known = left_relay[role][r][2 * left_slot[own + i]]
                    new = a_relay[role][r][extra_slot[own + i]]
                    left_plain[:, pick_rows(i, role, r), :] = jnp.where(
                        is_extra[own + i] == 1, new, known
                    )

                others(
                    lambda i: push(
                        left_plain.at[:, pick_rows(i, role, r)],
                        a_full.at[:, band_of(sender, r)],
                        a_pick_sem,
                        a_sem.at[role * bands + r],
                        own + i,
                    )
                )
                keep(
                    left_plain.at[:, pick_rows(place, role, r)],
                    a_full.at[:, band_of(sender, r)],
                    a_sem.at[role * bands + r],
                )

    landed(a_full.at[:, pl.ds(0, quarter * band)], a_sem.at[max(2 * bands - 2, 0)])
    for c in range(min(AHEAD, chunks)):
        pl.when(jnp.logical_not(is_relay))(functools.partial(cross_b, 0, c))

    def relay_right(role, c):
        landed(b_relay[role][c].at[pl.ds(0, extra)], b_relay_sem.at[role, c])
        across = pl.ds(c * width, width)

        @pl.loop(0, half)
        def _(i):
            for r in range(bands):
                down = pl.ds(r * band, band)
                known = left_relay[role][r][2 * left_slot[own + i] + 1, :, :, across]
                new = b_relay[role][c][extra_slot[own + i], :, down, :]
                b_pick[c, i, role, :, down, :] = jnp.where(is_extra[own + i] == 1, new, known)

        others(
            lambda i: push(
                b_pick.at[c, i, role],
                b_full.at[c, :, rows_of(senders[role])],
                b_pick_sem.at[c],
                b_sem.at[c],
                own + i,
            )
        )
        keep(
            b_pick.at[c, place, role], b_full.at[c, :, rows_of(senders[role])], b_sem.at[c]
        )

    @pl.when(is_relay)
    def _():
        for c in range(min(EARLY, chunks)):
            relay_right(1, c)

    landed(a_full.at[:, pl.ds(0, half * rows)], a_sem.at[2 * bands])
    for t in range(2 * bands):
        if t != 2 * bands - 2:
            landed(a_full.at[:, pl.ds(0, quarter * band)], a_sem.at[t])

    def each(c, step):
        for k in range(chunks):
            pl.when(c == k)(functools.partial(step, k))

    def all_far(c):
        def to_far(q):
            for j in range(2):
                push(
                    b_full.at[c, :, rows_of(other + j * quarter + q)],
                    relayed[c].at[place, j],
                    relay_out_sem.at[c],
                    relay_sem.at[c],
                    relays + q,
                )

        @pl.loop(1, quarter)
        def _(t):
            to_far(lax.rem(lane + t, quarter))

        @pl.when(is_relay)
        def _():
            for j, owner in enumerate(owners):
                keep(b_full.at[c, :, rows_of(owner)], relayed[c].at[place, j], relay_sem.at[c])

        @pl.when(jnp.logical_not(is_relay))
        def _():
            to_far(lane)

    def all_near(c):
        others(
            lambda i: push(
                b_full.at[c, :, rows_of(own + i)],
                panels[c].at[place],
                near_out_sem.at[c],
                near_sem.at[c],
                own + i,
            )
        )
        keep(b_full.at[c, :, my_rows], panels[c].at[place], near_sem.at[c])

    piece = min(TILE, order // 2)

    def compute(c):
        @pl.loop(0, tiles)
        def _(i):
            down = block(i)
            real_part, imag_part = tile_product(
                a_full[0, down, :], a_full[1, down, :], b_full[c, 0], b_full[c, 1]
            )
            right_pair[0, down, :] = real_part
            right_pair[1, down, :] = imag_part

        @pl.loop(0, order // piece)
        def _(i):
            start = lax.rem(other * rows + i * piece, order)
            down = pl.ds(pl.multiple_of(start, piece), piece)
            real_part, imag_part = tile_product(
                left_used[0, down, :], left_used[1, down, :], right_pair[0], right_pair[1]
            )
            b_full[c, 0, down, :] = real_part
            b_full[c, 1, down, :] = imag_part
            pl.when(i == order // piece // 2 - 1)(functools.partial(each, c, all_far))

    def merge(c):
        landed(relayed[c].at[near], relay_sem.at[c])

        @pl.loop(0, slots)
        def _(t):
            at = 2 * (side * most + t)
            first = relayed[c][merges[at]].astype(jnp.float32)
            second = relayed[c][merges[at + 1]].astype(jnp.float32)
            total = (first + second).astype(out.dtype)
            for j in range(2):
                b_relay[j][c][t] = total[j]

        for j, owner in enumerate(owners):
            push(
                b_relay[j][c].at[pl.ds(0, slots)],
                panels[c].at[far],
                far_out_sem.at[c],
                far_sem.at[c],
                owner,
            )

    pl.when(is_relay)(functools.partial(relay_right, 0, 0))

    def relay_next(c):
        if c + 1 < chunks:
            relay_right(0, c + 1)
        if c + EARLY < chunks:
            relay_right(1, c + EARLY)

    def cross_next(c):
        if c + AHEAD < chunks:
            cross_b(0, c + AHEAD)

    def merge_last(c):
        if c > 0:
            merge(c - 1)

    @pl.loop(0, chunks)
    def _(c):
        pl.when(is_relay)(functools.partial(each, c, relay_next))
        landed(b_full.at[c], b_sem.at[c])
        pl.when(jnp.logical_not(is_relay))(functools.partial(each, c, cross_next))
        compute(c)
        each(c, all_near)
        pl.when(is_relay)(functools.partial(each, c, merge_last))

    pl.when(is_relay)(functools.partial(merge, chunks - 1))

    for c in range(chunks):
        landed(panels[c].at[near], near_sem.at[c])
        landed(panels[c].at[far], far_sem.at[c])

        @pl.loop(0, out.shape[0])
        def _(d):
            at = 2 * (side * out.shape[0] + d)
            first = panels[c][finals[at]].astype(jnp.float32)
            second = panels[c][finals[at + 1]].astype(jnp.float32)
            out[d, :, :, c * width : (c + 1) * width] = (first + second).astype(out.dtype)

    rest = pl.ds(0, half - 1)
    landed(left_cross, left_cross_sem)
    landed(left_own.at[rest], left_out_sem)
    landed(a_cross.at[pl.ds(0, extra)], a_cross_sem)
    landed(a_own.at[rest], a_out_sem)
    for c in range(chunks):
        landed(b_cross.at[c, pl.ds(0, extra)], b_cross_sem.at[c])
        landed(b_own.at[c, rest], b_out_sem.at[c])
        landed(panels[c].at[rest], near_out_sem.at[c])
        landed(relayed[c].at[pl.ds(0, quarter - 1)], relay_out_sem.at[c])

    @pl.when(is_relay)
    def _():
        for role in range(2):
            for r in range(bands):
                landed(left_relay[role][r].at[rest], left_pick_sem)
                landed(left_relay[role][r].at[rest], a_pick_sem)
        for c in range(chunks):
            landed(b_pick.at[c, rest], b_pick_sem.at[c])
            for j in range(2):
                landed(b_relay[j][c].at[pl.ds(0, slots)], far_out_sem.at[c])

    @pl.when(jnp.logical_not(is_relay))
    def _():
        for c in range(chunks):
            landed(relayed[c].at[0], relay_out_sem.at[c])


def exchange(n, which, sizes, *rows_in):
    extra, slots = sizes
    *_, merges, _, left_own, _, b_own, _, _, _ = rows_in
    half, parts, rows, order = left_own.shape
    chunks, width = b_own.shape[0], b_own.shape[-1]
    most = merges.shape[0] // 4
    bands = rows // BAND
    sources = 2
    kind = left_own.dtype
    matrix = parts * order * order
    blocks = 4 * half + 2 * extra + 2 * max(extra, slots) + (half + most + 1) + 2 * (half + 1)
    held = 5 * matrix + parts * order * width + blocks * parts * rows * order
    dma = pltpu.SemaphoreType.DMA
    smem = pl.BlockSpec(memory_space=pltpu.SMEM)
    anywhere = pl.BlockSpec(memory_space=pl.ANY)
    return pl.pallas_call(
        functools.partial(exchange_kernel, n, slots),
        out_shape=jax.ShapeDtypeStruct((half, parts, rows, order), kind),
        in_specs=[smem] * 6 + [anywhere] * 6,
        out_specs=pl.BlockSpec(memory_space=pltpu.VMEM),
        scratch_shapes=[
            pltpu.VMEM((2, parts, order, order), kind),
            pltpu.VMEM((parts, order, order), kind),
            pltpu.VMEM((chunks, parts, order, width), kind),
            pltpu.VMEM((parts, order, order), kind),
            pltpu.VMEM((parts, order, width), kind),
            [[pltpu.VMEM((half, parts, BAND, order), kind)] * bands] * sources,
            [[pltpu.VMEM((extra, parts, BAND, order), kind)] * bands] * sources,
            [[pltpu.VMEM((max(extra, slots), parts, rows, width), kind)] * chunks] * sources,
            pltpu.VMEM((chunks, half, sources, parts, rows, width), kind),
            [pltpu.VMEM((half + most + 1, parts, rows, width), kind)] * chunks,
            [pltpu.VMEM((half + 1, sources, parts, rows, width), kind)] * chunks,
            dma,
            dma((2 * bands + 1,)),
            dma((chunks,)),
            dma,
            dma((sources, bands)),
            dma((sources, bands)),
            dma((sources, chunks)),
            dma((chunks,)),
            dma((chunks,)),
            dma((chunks,)),
            dma,
            dma,
            dma((chunks,)),
            dma,
            dma,
            dma,
            dma((chunks,)),
            dma,
            dma,
            dma((chunks,)),
            dma((chunks,)),
            dma((chunks,)),
            dma((chunks,)),
        ],
        compiler_params=pltpu.CompilerParams(
            collective_id=which,
            has_side_effects=True,
            vmem_limit_bytes=held * kind.itemsize + 2**20,
        ),
    )(*rows_in)


def local(nodes, pair_nodes, prod_left, prod_right, prod_flag, prod_diag, *, n):
    _, parts, rows, order = nodes.shape
    count = prod_left.shape[0]
    assert count == n == pair_nodes.shape[0] and rows * n == order and n % 4 == 0
    kind_of, *rows_in = plan_and_gather(
        n, nodes, pair_nodes, prod_left, prod_right, prod_flag, prod_diag, order // WIDTH
    )
    kernels = [
        functools.partial(exchange, n, which, sizes)
        for which, sizes in enumerate(plan_sizes(count))
    ]
    if len(kernels) == 1:
        return kernels[0](*rows_in)
    return lax.switch(kind_of[0], kernels, *rows_in)


def solution(mesh):
    placed = (P("grp", None, "node", None), P(), P(), P(), P(), P())
    return jax.shard_map(
        functools.partial(local, n=mesh.shape["node"]),
        mesh=mesh,
        in_specs=placed,
        out_specs=P("grp", None, "node", None),
        check_vma=False,
    )
```

```python
import functools

import jax
import jax.numpy as jnp
from jax import lax
from jax.experimental import pallas as pl
from jax.experimental.pallas import tpu as pltpu
from jax.sharding import PartitionSpec as P

TILE = 256
WIDTH = 128
EARLY = 2
AHEAD = 3
BAND = 16
LANES = 128


def searched(count):
    return 2 ** (count // 2 - 1) <= LANES


def plan_sizes(count):
    groups = count // 2
    if not searched(count):
        return [(groups, groups)]
    extra = slots = 3 * groups // 4
    return [(extra - 1, slots - 1), (extra - 1, slots), (extra, slots)]


def choose_sides(graph, product, home, sides, group_of):
    groups = sides.shape[0]
    count = 2 * groups
    half = groups
    lane = lax.broadcasted_iota(jnp.int32, sides.shape, 1)
    group = lax.broadcasted_iota(jnp.int32, sides.shape, 0)
    sides[...] = lax.rem(lax.shift_right_logical(lane, group), 2).astype(jnp.float32)
    row = lambda g: sides[pl.ds(g, 1), :]
    zero = jnp.zeros((1, sides.shape[1]), jnp.float32)

    def add_group(g, carry):
        ones, inside_0, inside_1 = carry
        here = row(g)
        there = row(group_of[home[graph[2, product[2 * g]]]])
        return ones + here, inside_0 + (1 - here) * (1 - there), inside_1 + here * there

    ones, inside_0, inside_1 = lax.fori_loop(0, groups, add_group, (zero, zero, zero))

    def add_diag(k, carry):
        own_0, own_1 = carry
        k_mate = product[count + k]
        here, there = row(group_of[k]), row(group_of[k_mate])
        first = (k < k_mate).astype(jnp.float32)
        return own_0 + first * (1 - here * there), own_1 + first * jnp.maximum(here, there)

    own_0, own_1 = lax.fori_loop(0, count, add_diag, (zero, zero))
    new = half - jnp.minimum(inside_0, inside_1)
    own = jnp.maximum(own_0, own_1)
    cost = jnp.full(new.shape, 64.0)
    sizes = plan_sizes(count)
    for index in reversed(range(len(sizes))):
        fits = (new <= sizes[index][0]) & (own <= sizes[index][1]) & (ones == groups // 2)
        cost = jnp.where(fits, float(index), cost)
    best = jnp.min(cost)
    index = lax.broadcasted_iota(jnp.int32, cost.shape, 1).astype(jnp.float32)
    mask = jnp.min(jnp.where(cost == best, index, 1e9)).astype(jnp.int32)
    return mask, jnp.minimum(best, float(len(sizes) - 1)).astype(jnp.int32)


def plan_and_gather_kernel(
    n,
    graph,
    nodes,
    kind_of,
    flags,
    left_slot,
    extra_slot,
    is_extra,
    merges,
    finals,
    left_own,
    a_own,
    b_own,
    left_cross,
    a_cross,
    b_cross,
    seen,
    group_of,
    product,
    home,
    chip_of,
    extras,
    used,
    slot_of,
    order,
    sides,
    early_sem,
    late_sem,
):
    count = graph.shape[1]
    groups = diags = half = count // 2
    extra = a_cross.shape[0]
    slots = merges.shape[0] // 4
    chunks = b_own.shape[0]
    width = b_own.shape[-1]
    first_node, prod_left, prod_right, prod_flag, prod_diag = 0, 2, 3, 4, 5
    me = lax.axis_index("node")
    side = lax.div(me, n // 2)

    @pl.loop(0, count)
    def _(p):
        seen[p] = -1
        seen[count + p] = -1
        chip_of[p] = -1

    @pl.loop(0, 2 * extra)
    def _(e):
        extras[e] = 0

    @pl.loop(0, 2 * diags)
    def _(d):
        slot_of[d] = -1

    def read(k, found):
        left = graph[prod_left, k]
        new = seen[left] < 0
        group = jnp.where(new, found, seen[left])
        seen[left] = group
        group_of[k] = group
        product[2 * group + 1] = k
        product[2 * group] = jnp.where(new, k, product[2 * group])
        home[graph[prod_right, k]] = k
        diag = graph[prod_diag, k]
        earlier = seen[count + diag]
        seen[count + diag] = k
        back = jnp.where(earlier < 0, k, earlier)
        product[count + k] = back
        product[count + back] = k
        return found + new.astype(jnp.int32)

    lax.fori_loop(0, count, read, jnp.int32(0))

    if not searched(count):
        mask, kind_of[0] = jnp.int32(2 ** (groups // 2) - 1), 0
    else:
        mask, kind_of[0] = choose_sides(graph, product, home, sides, group_of)

    def place(g, counts):
        which = lax.rem(lax.shift_right_logical(mask, g), 2)
        chip = jnp.where(which == 0, counts[0], groups // 2 + counts[1])
        order[2 * chip] = product[2 * g]
        order[2 * chip + 1] = product[2 * g + 1]
        chip_of[graph[prod_left, product[2 * g]]] = chip
        return counts[0] + 1 - which, counts[1] + which

    lax.fori_loop(0, groups, place, (jnp.int32(0), jnp.int32(0)))

    def read_node(node, dst, sem):
        pltpu.make_async_copy(nodes.at[node], dst, sem).start()

    def read_chunks(node, dst, at):
        for c in range(chunks):
            pltpu.make_async_copy(
                nodes.at[node, :, :, pl.ds(c * width, width)], dst.at[c, at], late_sem
            ).start()

    def left_node(k, at):
        return graph[lax.rem(at, 2), graph[prod_left, k]]

    @pl.loop(0, half)
    def _(i):
        read_node(left_node(order[(1 - side) * half + i], i), left_cross.at[i], early_sem)
        read_node(left_node(order[side * half + i], i), left_own.at[i], early_sem)

    used[0] = 0
    used[1] = 0

    @pl.loop(0, count)
    def _(at):
        which = lax.div(at, half)
        right = graph[prod_right, order[at]]
        chip = chip_of[right]
        local = (chip >= 0) & (lax.div(jnp.maximum(chip, 0), groups // 2) == which)
        spare = jnp.minimum(used[which], extra - 1)
        flags[at] = graph[prod_flag, order[at]]
        left_slot[at] = jnp.where(local, lax.rem(jnp.maximum(chip, 0), groups // 2), 0)
        extra_slot[at] = jnp.where(local, 0, spare)
        is_extra[at] = jnp.where(local, 0, 1)
        extras[which * extra + spare] = jnp.where(
            local, extras[which * extra + spare], right
        )
        used[which] = used[which] + jnp.where(local, 0, 1)

    @pl.loop(0, extra)
    def _(e):
        pair = extras[(1 - side) * extra + e]
        read_node(graph[first_node, pair], a_cross.at[e], early_sem)
        read_chunks(graph[first_node + 1, pair], b_cross, e)

    @pl.loop(0, half)
    def _(i):
        right = graph[prod_right, order[side * half + i]]
        read_node(graph[first_node, right], a_own.at[i], early_sem)
        read_chunks(graph[first_node + 1, right], b_own, i)

    for h in range(2):
        base = h * slots

        @pl.loop(0, slots)
        def _(t):
            merges[2 * (base + t)] = half
            merges[2 * (base + t) + 1] = half

        def take(i, taken):
            diag = graph[prod_diag, order[h * half + i]]
            slot = slot_of[h * diags + diag]
            new = slot < 0
            slot = jnp.where(new, jnp.minimum(taken, slots - 1), slot)
            slot_of[h * diags + diag] = slot
            at = 2 * (base + slot)
            merges[at] = jnp.where(new, i, merges[at])
            merges[at + 1] = jnp.where(new, half, i)
            return taken + new.astype(jnp.int32)

        lax.fori_loop(0, half, take, jnp.int32(0))

    for h in range(2):

        @pl.loop(0, diags)
        def _(d):
            near = slot_of[h * diags + d]
            far = half + slot_of[(1 - h) * diags + d]
            here = near >= 0
            at = 2 * (h * slots + jnp.maximum(near, 0))
            both = here & (merges[at + 1] < half)
            finals[2 * (h * diags + d)] = jnp.where(here, merges[at], far)
            finals[2 * (h * diags + d) + 1] = jnp.where(
                both, merges[at + 1], jnp.where(here, far, half + slots)
            )

    for ref in (left_own, a_own, left_cross, a_cross):
        pltpu.make_async_copy(ref, ref, early_sem).wait()
    for ref in (b_own, b_cross):
        pltpu.make_async_copy(ref, ref, late_sem).wait()


def plan_and_gather(n, nodes, pair_nodes, prod_left, prod_right, prod_flag, prod_diag, chunks):
    count = prod_left.shape[0]
    _, parts, rows, order = nodes.shape
    half = groups = count // 2
    extra, slots = plan_sizes(count)[-1]
    width = order // chunks
    graph = jnp.stack(
        [pair_nodes[:, 0], pair_nodes[:, 1], prod_left, prod_right, prod_flag, prod_diag]
    )
    whole = lambda size: jax.ShapeDtypeStruct((size, parts, rows, order), nodes.dtype)
    cut = lambda size: jax.ShapeDtypeStruct((chunks, size, parts, rows, width), nodes.dtype)
    table = lambda size: jax.ShapeDtypeStruct((size,), jnp.int32)
    smem = pl.BlockSpec(memory_space=pltpu.SMEM)
    scratch = lambda size: pltpu.SMEM((size,), jnp.int32)
    return pl.pallas_call(
        functools.partial(plan_and_gather_kernel, n),
        out_shape=(
            table(1),
            table(count),
            table(count),
            table(count),
            table(count),
            table(4 * slots),
            table(4 * half),
            whole(half),
            whole(half),
            cut(half),
            whole(half),
            whole(extra),
            cut(extra),
        ),
        in_specs=[smem, pl.BlockSpec(memory_space=pltpu.HBM)],
        out_specs=[smem] * 7 + [pl.BlockSpec(memory_space=pltpu.VMEM)] * 6,
        scratch_shapes=[
            scratch(2 * count),
            scratch(count),
            scratch(2 * count),
            scratch(count),
            scratch(count),
            scratch(2 * extra),
            scratch(2),
            scratch(2 * half),
            scratch(count),
            pltpu.VMEM((groups, LANES), jnp.float32),
            pltpu.SemaphoreType.DMA,
            pltpu.SemaphoreType.DMA,
        ],
        compiler_params=pltpu.CompilerParams(vmem_limit_bytes=50 * 2**20),
    )(graph, nodes)


def tile_product(left_re, left_im, right_re, right_im):
    dot = functools.partial(jnp.dot, preferred_element_type=jnp.float32)
    real_part = dot(left_re, right_re) - dot(left_im, right_im)
    imag_part = dot(left_re, right_im) + dot(left_im, right_re)
    return real_part.astype(jnp.bfloat16), imag_part.astype(jnp.bfloat16)


def exchange_kernel(
    n,
    slots,
    flags,
    left_slot,
    extra_slot,
    is_extra,
    merges,
    finals,
    left_own,
    a_own,
    b_own,
    left_cross,
    a_cross,
    b_cross,
    out,
    lefts,
    a_full,
    b_full,
    left_plain,
    right_pair,
    left_relay,
    a_relay,
    b_relay,
    b_pick,
    panels,
    relayed,
    left_sem,
    a_sem,
    b_sem,
    swap_sem,
    left_relay_sem,
    a_relay_sem,
    b_relay_sem,
    near_sem,
    relay_sem,
    far_sem,
    left_out_sem,
    a_out_sem,
    b_out_sem,
    swap_out_sem,
    left_cross_sem,
    a_cross_sem,
    b_cross_sem,
    left_pick_sem,
    a_pick_sem,
    b_pick_sem,
    near_out_sem,
    relay_out_sem,
    far_out_sem,
):
    me = lax.axis_index("node")
    parity = lax.rem(me, 2)
    partner = me + 1 - 2 * parity
    chunks, _, order, width = b_full.shape
    rows = left_own.shape[2]
    half, quarter = n // 2, n // 4
    extra = a_relay[0][0].shape[0]
    bands = len(left_relay[0])
    band = rows // bands
    tiles = order // TILE
    side, place = lax.div(me, half), lax.rem(me, half)
    own, other = side * half, (1 - side) * half
    lane, hop = lax.rem(me, quarter), lax.div(place, quarter)
    relays = quarter + side * (half - quarter)
    to_relay = half - side * (half - quarter) + lane
    is_relay = hop + side == 1

    barrier = pltpu.get_barrier_semaphore()

    def greet(device):
        pl.semaphore_signal(
            barrier, inc=1, device_id={"node": device}, device_id_type=pl.DeviceIdType.MESH
        )

    @pl.loop(1, half)
    def _(t):
        greet(own + lax.rem(place + t, half))

    greet(to_relay)

    @pl.when(is_relay)
    def _():
        greet(other + (1 - side) * quarter + lane)

    pl.semaphore_wait(barrier, half + jnp.where(is_relay, 1, 0))

    def push(src, dst, send_sem, recv_sem, to):
        pltpu.make_async_remote_copy(
            src_ref=src,
            dst_ref=dst,
            send_sem=send_sem,
            recv_sem=recv_sem,
            device_id={"node": to},
            device_id_type=pl.DeviceIdType.MESH,
        ).start()

    def keep(src, dst, sem):
        pltpu.make_async_copy(src, dst, sem).start()

    def landed(ref, sem):
        pltpu.make_async_copy(ref, ref, sem).wait()

    def rows_of(device):
        return pl.ds(pl.multiple_of(device * rows, rows), rows)

    def band_of(device, r):
        return pl.ds(pl.multiple_of(device * rows + r * band, band), band)

    my_rows = rows_of(me)
    most = merges.shape[0] // 4
    near, far = pl.ds(0, half), pl.ds(half, slots)
    owners = [other + lane, other + quarter + lane]
    senders = [other + (1 - side) * quarter + lane, other + side * quarter + lane]

    def by_role(step):
        pl.when(jnp.logical_not(is_relay))(functools.partial(step, 0))
        pl.when(is_relay)(functools.partial(step, 1))

    def others(step):
        @pl.loop(1, half)
        def _(t):
            step(lax.rem(place + t, half))

    def cross_left(role):
        for r in range(bands):
            push(
                left_cross.at[:, :, pl.ds(r * band, band)],
                left_relay[role][r],
                left_cross_sem,
                left_relay_sem.at[role, r],
                to_relay,
            )

    def cross_a(role):
        for r in range(bands):
            push(
                a_cross.at[pl.ds(0, extra), :, pl.ds(r * band, band)],
                a_relay[role][r],
                a_cross_sem,
                a_relay_sem.at[role, r],
                to_relay,
            )

    def cross_b(role, c):
        push(
            b_cross.at[c, pl.ds(0, extra)],
            b_relay[role][c].at[pl.ds(0, extra)],
            b_cross_sem.at[c],
            b_relay_sem.at[role, c],
            to_relay,
        )

    def share_b(c):
        others(
            lambda i: push(
                b_own.at[c, i], b_full.at[c, :, my_rows], b_out_sem.at[c], b_sem.at[c], own + i
            )
        )
        keep(b_own.at[c, place], b_full.at[c, :, my_rows], b_sem.at[c])

    def share_left():
        others(
            lambda i: push(
                left_own.at[i],
                lefts.at[lax.rem(i, 2), :, my_rows],
                left_out_sem,
                left_sem,
                own + i,
            )
        )
        keep(left_own.at[place], lefts.at[parity, :, my_rows], left_sem)

    def share_a():
        others(
            lambda i: push(
                a_own.at[i], a_full.at[:, my_rows], a_out_sem, a_sem.at[2 * bands], own + i
            )
        )
        keep(a_own.at[place], a_full.at[:, my_rows], a_sem.at[2 * bands])

    by_role(cross_left)
    share_left()
    share_a()
    by_role(cross_a)

    @pl.when(jnp.logical_not(is_relay))
    def _():
        for c in range(chunks):
            share_b(c)

    for c in range(chunks):
        pl.when(is_relay)(functools.partial(cross_b, 1, c))

    for c in range(chunks):
        for unused in range(slots, most + 1):
            panels[c][half + unused] = jnp.zeros(panels[c].shape[1:], panels[c].dtype)
        relayed[c][half] = jnp.zeros(relayed[c].shape[1:], relayed[c].dtype)

    @pl.when(is_relay)
    def _():
        for role, sender in enumerate(senders):
            for r in range(bands):
                landed(left_relay[role][r], left_relay_sem.at[role, r])
                others(
                    lambda i: push(
                        left_relay[role][r].at[i],
                        lefts.at[lax.rem(i, 2), :, band_of(sender, r)],
                        left_pick_sem,
                        left_sem,
                        own + i,
                    )
                )
                keep(
                    left_relay[role][r].at[place],
                    lefts.at[parity, :, band_of(sender, r)],
                    left_sem,
                )
        for c in range(chunks):
            share_b(c)

    landed(lefts.at[parity], left_sem)

    push(lefts.at[parity], lefts.at[parity], swap_out_sem, swap_sem, partner)
    landed(lefts.at[1 - parity], swap_sem)

    def block(i):
        return pl.ds(pl.multiple_of(i * TILE, TILE), TILE)

    @pl.loop(0, tiles * tiles)
    def _(t):
        down, across = block(lax.div(t, tiles)), block(lax.rem(t, tiles))
        real_part, imag_part = tile_product(
            lefts[0, 0, down, :], lefts[0, 1, down, :], lefts[1, 0, :, across], lefts[1, 1, :, across]
        )
        left_plain[0, down, across] = real_part
        left_plain[1, down, across] = imag_part

    landed(lefts.at[parity], swap_out_sem)
    left_used = lefts.at[0]
    flipped = flags[me] == 1

    @pl.loop(0, tiles * tiles)
    def _(t):
        down, across = block(lax.div(t, tiles)), block(lax.rem(t, tiles))
        left_used[0, down, across] = jnp.where(
            flipped, left_plain[0, across, down].T, left_plain[0, down, across]
        )
        left_used[1, down, across] = jnp.where(
            flipped, -left_plain[1, across, down].T, left_plain[1, down, across]
        )

    def pick_rows(i, role, r):
        return pl.ds(pl.multiple_of((2 * i + role) * rows + r * band, band), band)

    @pl.when(is_relay)
    def _():
        for role, sender in enumerate(senders):
            for r in range(bands):
                landed(a_relay[role][r], a_relay_sem.at[role, r])

                @pl.loop(0, half)
                def _(i):
                    known = left_relay[role][r][2 * left_slot[own + i]]
                    new = a_relay[role][r][extra_slot[own + i]]
                    left_plain[:, pick_rows(i, role, r), :] = jnp.where(
                        is_extra[own + i] == 1, new, known
                    )

                others(
                    lambda i: push(
                        left_plain.at[:, pick_rows(i, role, r)],
                        a_full.at[:, band_of(sender, r)],
                        a_pick_sem,
                        a_sem.at[role * bands + r],
                        own + i,
                    )
                )
                keep(
                    left_plain.at[:, pick_rows(place, role, r)],
                    a_full.at[:, band_of(sender, r)],
                    a_sem.at[role * bands + r],
                )

    landed(a_full.at[:, pl.ds(0, quarter * band)], a_sem.at[max(2 * bands - 2, 0)])
    for c in range(min(AHEAD, chunks)):
        pl.when(jnp.logical_not(is_relay))(functools.partial(cross_b, 0, c))

    def relay_right(role, c):
        landed(b_relay[role][c].at[pl.ds(0, extra)], b_relay_sem.at[role, c])
        across = pl.ds(c * width, width)

        @pl.loop(0, half)
        def _(i):
            for r in range(bands):
                down = pl.ds(r * band, band)
                known = left_relay[role][r][2 * left_slot[own + i] + 1, :, :, across]
                new = b_relay[role][c][extra_slot[own + i], :, down, :]
                b_pick[c, i, role, :, down, :] = jnp.where(is_extra[own + i] == 1, new, known)

        others(
            lambda i: push(
                b_pick.at[c, i, role],
                b_full.at[c, :, rows_of(senders[role])],
                b_pick_sem.at[c],
                b_sem.at[c],
                own + i,
            )
        )
        keep(
            b_pick.at[c, place, role], b_full.at[c, :, rows_of(senders[role])], b_sem.at[c]
        )

    @pl.when(is_relay)
    def _():
        for c in range(min(EARLY, chunks)):
            relay_right(1, c)

    landed(a_full.at[:, pl.ds(0, half * rows)], a_sem.at[2 * bands])
    for t in range(2 * bands):
        if t != 2 * bands - 2:
            landed(a_full.at[:, pl.ds(0, quarter * band)], a_sem.at[t])

    def each(c, step):
        for k in range(chunks):
            pl.when(c == k)(functools.partial(step, k))

    def all_far(c):
        def to_far(q):
            for j in range(2):
                push(
                    b_full.at[c, :, rows_of(other + j * quarter + q)],
                    relayed[c].at[place, j],
                    relay_out_sem.at[c],
                    relay_sem.at[c],
                    relays + q,
                )

        @pl.loop(1, quarter)
        def _(t):
            to_far(lax.rem(lane + t, quarter))

        @pl.when(is_relay)
        def _():
            for j, owner in enumerate(owners):
                keep(b_full.at[c, :, rows_of(owner)], relayed[c].at[place, j], relay_sem.at[c])

        @pl.when(jnp.logical_not(is_relay))
        def _():
            to_far(lane)

    def all_near(c):
        others(
            lambda i: push(
                b_full.at[c, :, rows_of(own + i)],
                panels[c].at[place],
                near_out_sem.at[c],
                near_sem.at[c],
                own + i,
            )
        )
        keep(b_full.at[c, :, my_rows], panels[c].at[place], near_sem.at[c])

    piece = min(TILE, order // 2)

    def compute(c):
        @pl.loop(0, tiles)
        def _(i):
            down = block(i)
            real_part, imag_part = tile_product(
                a_full[0, down, :], a_full[1, down, :], b_full[c, 0], b_full[c, 1]
            )
            right_pair[0, down, :] = real_part
            right_pair[1, down, :] = imag_part

        @pl.loop(0, order // piece)
        def _(i):
            start = lax.rem(other * rows + i * piece, order)
            down = pl.ds(pl.multiple_of(start, piece), piece)
            real_part, imag_part = tile_product(
                left_used[0, down, :], left_used[1, down, :], right_pair[0], right_pair[1]
            )
            b_full[c, 0, down, :] = real_part
            b_full[c, 1, down, :] = imag_part
            pl.when(i == order // piece // 2 - 1)(functools.partial(each, c, all_far))

    def merge(c):
        landed(relayed[c].at[near], relay_sem.at[c])

        @pl.loop(0, slots)
        def _(t):
            at = 2 * (side * most + t)
            first = relayed[c][merges[at]].astype(jnp.float32)
            second = relayed[c][merges[at + 1]].astype(jnp.float32)
            total = (first + second).astype(out.dtype)
            for j in range(2):
                b_relay[j][c][t] = total[j]

        for j, owner in enumerate(owners):
            push(
                b_relay[j][c].at[pl.ds(0, slots)],
                panels[c].at[far],
                far_out_sem.at[c],
                far_sem.at[c],
                owner,
            )

    pl.when(is_relay)(functools.partial(relay_right, 0, 0))

    def relay_next(c):
        if c + 1 < chunks:
            relay_right(0, c + 1)
        if c + EARLY < chunks:
            relay_right(1, c + EARLY)

    def cross_next(c):
        if c + AHEAD < chunks:
            cross_b(0, c + AHEAD)

    def merge_last(c):
        if c > 0:
            merge(c - 1)

    @pl.loop(0, chunks)
    def _(c):
        pl.when(is_relay)(functools.partial(each, c, relay_next))
        landed(b_full.at[c], b_sem.at[c])
        pl.when(jnp.logical_not(is_relay))(functools.partial(each, c, cross_next))
        compute(c)
        each(c, all_near)
        pl.when(is_relay)(functools.partial(each, c, merge_last))

    pl.when(is_relay)(functools.partial(merge, chunks - 1))

    for c in range(chunks):
        landed(panels[c].at[near], near_sem.at[c])
        landed(panels[c].at[far], far_sem.at[c])

        @pl.loop(0, out.shape[0])
        def _(d):
            at = 2 * (side * out.shape[0] + d)
            first = panels[c][finals[at]].astype(jnp.float32)
            second = panels[c][finals[at + 1]].astype(jnp.float32)
            out[d, :, :, c * width : (c + 1) * width] = (first + second).astype(out.dtype)

    rest = pl.ds(0, half - 1)
    landed(left_cross, left_cross_sem)
    landed(left_own.at[rest], left_out_sem)
    landed(a_cross.at[pl.ds(0, extra)], a_cross_sem)
    landed(a_own.at[rest], a_out_sem)
    for c in range(chunks):
        landed(b_cross.at[c, pl.ds(0, extra)], b_cross_sem.at[c])
        landed(b_own.at[c, rest], b_out_sem.at[c])
        landed(panels[c].at[rest], near_out_sem.at[c])
        landed(relayed[c].at[pl.ds(0, quarter - 1)], relay_out_sem.at[c])

    @pl.when(is_relay)
    def _():
        for role in range(2):
            for r in range(bands):
                landed(left_relay[role][r].at[rest], left_pick_sem)
                landed(left_relay[role][r].at[rest], a_pick_sem)
        for c in range(chunks):
            landed(b_pick.at[c, rest], b_pick_sem.at[c])
            for j in range(2):
                landed(b_relay[j][c].at[pl.ds(0, slots)], far_out_sem.at[c])

    @pl.when(jnp.logical_not(is_relay))
    def _():
        for c in range(chunks):
            landed(relayed[c].at[0], relay_out_sem.at[c])


def exchange(n, which, sizes, *rows_in):
    extra, slots = sizes
    *_, merges, _, left_own, _, b_own, _, _, _ = rows_in
    half, parts, rows, order = left_own.shape
    chunks, width = b_own.shape[0], b_own.shape[-1]
    most = merges.shape[0] // 4
    bands = rows // BAND
    sources = 2
    kind = left_own.dtype
    matrix = parts * order * order
    blocks = 4 * half + 2 * extra + 2 * max(extra, slots) + (half + most + 1) + 2 * (half + 1)
    held = 5 * matrix + parts * order * width + blocks * parts * rows * order
    dma = pltpu.SemaphoreType.DMA
    smem = pl.BlockSpec(memory_space=pltpu.SMEM)
    anywhere = pl.BlockSpec(memory_space=pl.ANY)
    return pl.pallas_call(
        functools.partial(exchange_kernel, n, slots),
        out_shape=jax.ShapeDtypeStruct((half, parts, rows, order), kind),
        in_specs=[smem] * 6 + [anywhere] * 6,
        out_specs=pl.BlockSpec(memory_space=pltpu.VMEM),
        scratch_shapes=[
            pltpu.VMEM((2, parts, order, order), kind),
            pltpu.VMEM((parts, order, order), kind),
            pltpu.VMEM((chunks, parts, order, width), kind),
            pltpu.VMEM((parts, order, order), kind),
            pltpu.VMEM((parts, order, width), kind),
            [[pltpu.VMEM((half, parts, BAND, order), kind)] * bands] * sources,
            [[pltpu.VMEM((extra, parts, BAND, order), kind)] * bands] * sources,
            [[pltpu.VMEM((max(extra, slots), parts, rows, width), kind)] * chunks] * sources,
            pltpu.VMEM((chunks, half, sources, parts, rows, width), kind),
            [pltpu.VMEM((half + most + 1, parts, rows, width), kind)] * chunks,
            [pltpu.VMEM((half + 1, sources, parts, rows, width), kind)] * chunks,
            dma,
            dma((2 * bands + 1,)),
            dma((chunks,)),
            dma,
            dma((sources, bands)),
            dma((sources, bands)),
            dma((sources, chunks)),
            dma((chunks,)),
            dma((chunks,)),
            dma((chunks,)),
            dma,
            dma,
            dma((chunks,)),
            dma,
            dma,
            dma,
            dma((chunks,)),
            dma,
            dma,
            dma((chunks,)),
            dma((chunks,)),
            dma((chunks,)),
            dma((chunks,)),
        ],
        compiler_params=pltpu.CompilerParams(
            collective_id=which,
            has_side_effects=True,
            vmem_limit_bytes=held * kind.itemsize + 2**20,
        ),
    )(*rows_in)


def local(nodes, pair_nodes, prod_left, prod_right, prod_flag, prod_diag, *, n):
    _, parts, rows, order = nodes.shape
    count = prod_left.shape[0]
    assert count == n == pair_nodes.shape[0] and rows * n == order and n % 4 == 0
    kind_of, *rows_in = plan_and_gather(
        n, nodes, pair_nodes, prod_left, prod_right, prod_flag, prod_diag, order // WIDTH
    )
    kernels = [
        functools.partial(exchange, n, which, sizes)
        for which, sizes in enumerate(plan_sizes(count))
    ]
    if len(kernels) == 1:
        return kernels[0](*rows_in)
    return lax.switch(kind_of[0], kernels, *rows_in)


def solution(mesh):
    placed = (P("grp", None, "node", None), P(), P(), P(), P(), P())
    return jax.shard_map(
        functools.partial(local, n=mesh.shape["node"]),
        mesh=mesh,
        in_specs=placed,
        out_specs=P("grp", None, "node", None),
        check_vma=False,
    )
```
